256 devices in a mesh: dp: 4 (over y), expert: 64 (over x, z, core).
Axes of the slice: x: 4, y: 4, z: 8, core: 2. Of those that a mesh axis runs over, the one named last changes fastest.
Arguments:
- unit_codes: bfloat16 [128, 256, 1536], P('expert', 'dp'), may hold values from -4 to 4
- block_scales: float32 [128, 12, 256], P('expert', None, 'dp'), may hold values from 0.05 to 2
- pair_list: int32 [2048, 2], replicated, may hold values from 0 to 127, as said below
Outputs:
- left_best: float32 [64, 32, 1536], P('expert', None, 'dp')
- right_best: float32 [64, 32, 1536], P('expert', None, 'dp')
The draws below stay inside these ranges and needn't reach their ends.
Inputs may be any that keep to these rules, and one draw needn't show every extreme that they name: `pair_list`: row 32 * e + s names as its first expert one of 2 * e to 2 * e + 1, and as its second one of the 2 experts starting at 2 * ((e + o_s) mod n), with n = 64; the offsets o_s are nonzero, distinct over s, include 1, n / 2 and n - 1, and are the same for every e.
All inputs are finite; a program needn't handle non-finite values.
Results may differ from the reference program's by a relative error of at most 0.0017.
Values may be sent and summed in bfloat16 or wider, within the bound.
No kernel may reach another device: no remote copies, remote signals or barrier semaphores. Data moves between devices by JAX's collectives and lax.ppermute only.
A program may use at most 128 MiB of HBM per device.

```python
import math
import jax
import jax.numpy as jnp
from jax import lax

FF = 1536
EXP_DEV = 2
SCALE_BLOCK = 128
EXPERTS = 128
CAL_ROWS = 256
PAIR_DEV = 32
PAIRS = 2048
N_EXPERT = 64


def draw_pair_list(key, part):
    num_devices = EXPERTS // EXP_DEV
    key_offsets = jax.random.fold_in(key, 11)
    key_left = jax.random.fold_in(key, 12)
    key_right = jax.random.fold_in(key, 13)
    key_order = jax.random.fold_in(key, 14)
    values = jnp.arange(1, num_devices, dtype=jnp.int32)
    ranks = jax.random.permutation(key_offsets, num_devices - 1).astype(jnp.int32)
    ranks = jnp.where(values == 1, -3, ranks)
    ranks = jnp.where(values == num_devices // 2, -2, ranks)
    ranks = jnp.where(values == num_devices - 1, -1, ranks)
    order = jnp.argsort(ranks, stable=True)
    picked = jnp.take(values, order[:PAIR_DEV])
    offsets = jax.random.permutation(key_order, picked)
    device_ids = jnp.arange(num_devices, dtype=jnp.int32)[:, None]
    left_pick = jax.random.randint(key_left, (num_devices, PAIR_DEV), 0, EXP_DEV)
    left_pick = left_pick.at[:, 0].set(0).at[:, 1].set(EXP_DEV - 1)
    right_pick = jax.random.randint(key_right, (num_devices, PAIR_DEV), 0, EXP_DEV)
    first_expert = device_ids * EXP_DEV + left_pick
    second_expert = (device_ids + offsets[None, :]) % num_devices * EXP_DEV + right_pick
    stacked = jnp.stack([first_expert, second_expert], axis=-1)
    return stacked.reshape(PAIRS, 2).astype(jnp.int32)


def block_scale(own_key, extent, pieces, low, top_value):
    level = 1.0
    for axis_at, blocks in pieces:
        draws = jax.random.uniform(jax.random.fold_in(jax.random.fold_in(own_key, 6), axis_at), (blocks,), jnp.float32, low / len(pieces), top_value / len(pieces))
        level = level * jnp.repeat(jnp.exp(draws), extent[axis_at] // blocks).reshape((-1,) + (1,) * (len(extent) - 1 - axis_at))
    return level


def scatter_about(rng, shape, deviation, limit, cuts=(), held_as=jnp.bfloat16):
    entries = deviation * jax.random.normal(rng, shape, jnp.float32)
    if cuts:
        entries = entries * block_scale(rng, shape, cuts, -0.22, 0.18)
    return jnp.clip(entries, -limit, limit).astype(held_as)


def setup_inputs(seed: int = 0) -> dict:
    key_list = jax.random.split(jax.random.key(seed), 4)
    return {
        "unit_codes": scatter_about(key_list[0], (EXPERTS, CAL_ROWS, FF), 1.0, 4.0, ((0, 64), (1, 4))),
        "block_scales": jnp.clip(jnp.exp(math.log(2.0) - 3.6888794 * jax.random.uniform(key_list[1], (EXPERTS, FF // SCALE_BLOCK, CAL_ROWS), jnp.float32) ** block_scale(key_list[1], (EXPERTS, FF // SCALE_BLOCK, CAL_ROWS), ((0, 64), (2, 4)), -0.2, 0.2)), 0.05, 2.0),
        "pair_list": draw_pair_list(jax.random.fold_in(key_list[3], 71), 0),
    }


EPSILON = 1e-06

def reference(unit_codes, block_scales, pair_list):
    expanded = jnp.repeat(jnp.transpose(block_scales, (0, 2, 1)), SCALE_BLOCK, axis=2)
    acts = (unit_codes.astype(jnp.float32) * expanded).astype(jnp.bfloat16)
    acts_wide = acts.astype(jnp.float32)
    mean_square = lax.optimization_barrier(jnp.mean(acts_wide * acts_wide, axis=1))
    inverse = 1.0 / jnp.sqrt(mean_square + EPSILON)

    def single(pair_row):
        first_expert = pair_row[0]
        second_expert = pair_row[1]
        first_rows = jnp.take(acts_wide, first_expert, axis=0)
        second_rows = jnp.take(acts_wide, second_expert, axis=0)
        products = jnp.dot(first_rows.T, second_rows, precision=lax.Precision.HIGHEST, preferred_element_type=jnp.float32)
        correlation = products / CAL_ROWS * jnp.take(inverse, first_expert, axis=0)[:, None] * jnp.take(inverse, second_expert, axis=0)[None, :]
        return (lax.optimization_barrier(jnp.max(correlation, axis=1)), lax.optimization_barrier(jnp.max(correlation, axis=0)))
    left_rows, right_rows = lax.map(single, pair_list)
    left_best = left_rows.reshape(N_EXPERT, PAIR_DEV, FF)
    offsets = pair_list[:PAIR_DEV, 1] // EXP_DEV
    devices = jnp.arange(N_EXPERT, dtype=jnp.int32)[:, None]
    source_dev = (devices - offsets[None, :]) % N_EXPERT
    lookup = (source_dev * PAIR_DEV + jnp.arange(PAIR_DEV, dtype=jnp.int32)[None, :]).astype(jnp.int32)
    right_best = jnp.take(right_rows, lookup.reshape(-1), axis=0).reshape(N_EXPERT, PAIR_DEV, FF)
    return (left_best, right_best)
```

```python
import math

import jax
import jax.numpy as jnp
import numpy as np
from jax import lax
from jax.experimental import pallas as pl
from jax.experimental.pallas import tpu as pltpu
from jax.sharding import Mesh
from jax.sharding import PartitionSpec as P

EPSILON = 1e-06

NX, NZ, NC, NY = 4, 8, 2, 4
NDEV = NX * NZ * NC
PER = 2
ROWS = 256
RB = ROWS // NY
UNITS = 1536
SLICES = NX * NY
WIDTH = UNITS // SLICES
QUARTER = UNITS // NY
SLOTS = 32
PAIRS = NX * SLOTS
LEFTS = NX * PER
BLOCK = 128
GROUP = 8
TILE = 256

VMEM = pl.BlockSpec(memory_space=pltpu.VMEM)
ANY = pl.BlockSpec(memory_space=pl.ANY)


def prepare(codes, scales):
    def kernel(codes_ref, scales_ref, acts_ref, slices_ref):
        column = [jnp.transpose(scales_ref[h]) for h in range(PER)]
        for k in range(UNITS // BLOCK):
            lanes = slice(k * BLOCK, (k + 1) * BLOCK)
            both = []
            for h in range(PER):
                value = codes_ref[h, :, lanes].astype(jnp.float32) * column[h][:, k : k + 1]
                rounded = value.astype(jnp.bfloat16)
                acts_ref[h, :, lanes] = rounded
                both.append(rounded.astype(jnp.float32))
            turned = jnp.transpose(jnp.concatenate(both, axis=0)).astype(jnp.bfloat16)
            done = 0
            while done < BLOCK:
                unit = k * BLOCK + done
                take = min(BLOCK - done, WIDTH - unit % WIDTH)
                slices_ref[unit // WIDTH, unit % WIDTH : unit % WIDTH + take, :] = turned[
                    done : done + take
                ]
                done += take

    return pl.pallas_call(
        kernel,
        in_specs=[VMEM, VMEM],
        out_specs=[VMEM, VMEM],
        out_shape=[
            jax.ShapeDtypeStruct((PER, RB, UNITS), jnp.bfloat16),
            jax.ShapeDtypeStruct((SLICES, WIDTH, PER * RB), jnp.bfloat16),
        ],
        name="prepare",
    )(codes, scales)


def normalise(pieces):
    def kernel(in_ref, out_ref):
        for x in range(NX):
            part = [in_ref[y * NX + x].astype(jnp.float32) for y in range(NY)]
            for h in range(PER):
                lanes = slice(h * RB, (h + 1) * RB)
                full = jnp.concatenate([p[:, lanes] for p in part], axis=1)
                square = jnp.sum(full * full, axis=1, keepdims=True) / ROWS
                inverse = 1.0 / jnp.sqrt(square + EPSILON)
                out_ref[x * PER + h] = (full * (inverse * (1.0 / ROWS))).astype(jnp.bfloat16)

    return pl.pallas_call(
        kernel,
        in_specs=[VMEM],
        out_specs=VMEM,
        out_shape=jax.ShapeDtypeStruct((LEFTS, WIDTH, ROWS), jnp.bfloat16),
        name="normalise",
    )(pieces)


def correlate(start, order, jidx, lpos, rpos, gathered, chunks, places):
    count = len(chunks)

    def kernel(start_ref, order_ref, jidx_ref, lpos_ref, rpos_ref, *refs):
        gathered_ref = refs[0]
        chunk_refs = refs[1 : 1 + count]
        left_ref, right_ref, acts, others, inv, sem = refs[1 + count :]
        copies = []
        for x in range(NX):
            for y in range(NY):
                copies.append(
                    pltpu.make_async_copy(
                        gathered_ref.at[x * NY + y],
                        acts.at[pl.ds(x * PER, PER), pl.ds(y * RB, RB), :],
                        sem.at[len(copies)],
                    )
                )
        for ref, (at, size) in zip(chunk_refs, places):
            copies.append(
                pltpu.make_async_copy(ref, others.at[pl.ds(at, size)], sem.at[len(copies)])
            )
        for copy in copies:
            copy.start()
        right_ref[...] = jnp.zeros_like(right_ref)
        for copy in copies[: NX * NY]:
            copy.wait()

        def norm(i, carry):
            for n in range(UNITS // TILE):
                lanes = slice(n * TILE, (n + 1) * TILE)
                value = acts[i, :, lanes].astype(jnp.float32)
                square = jnp.sum(value * value, axis=0, keepdims=True) / ROWS
                inv[pl.ds(i, 1), lanes] = 1.0 / jnp.sqrt(square + EPSILON)
            return carry

        lax.fori_loop(0, LEFTS, norm, 0)
        for copy in copies[NX * NY :]:
            copy.wait()

        def expert(i, carry):
            low = start_ref[i]
            high = start_ref[i + 1]
            scales = inv[pl.ds(i, 1), :]

            def block(b, carry):
                pairs = [
                    order_ref[jnp.minimum(low + b * GROUP + g, high - 1)] for g in range(GROUP)
                ]
                lhs = jnp.concatenate([others[jidx_ref[p]] for p in pairs], axis=0)
                best = [None] * GROUP
                tops = [[] for _ in range(GROUP)]
                for n in range(UNITS // TILE):
                    out = jnp.dot(
                        lhs,
                        acts[i, :, n * TILE : (n + 1) * TILE],
                        preferred_element_type=jnp.float32,
                    )
                    for g in range(GROUP):
                        one = out[g * WIDTH : (g + 1) * WIDTH]
                        for m in range(TILE // 128):
                            unit = n * TILE + m * 128
                            scale = scales[:, unit : unit + 128]
                            part = one[:, m * 128 : (m + 1) * 128]
                            tops[g].append(jnp.max(part, axis=0, keepdims=True) * scale)
                            if (unit + 128) % QUARTER == 0:
                                row = lpos_ref[pairs[g]] + (unit // QUARTER) * SLOTS
                                left_ref[pl.ds(row, 1), :] = jnp.concatenate(tops[g], axis=1)
                                tops[g] = []
                            scaled = part * scale
                            best[g] = scaled if best[g] is None else jnp.maximum(best[g], scaled)
                for g in range(GROUP):
                    top = jnp.max(jnp.transpose(best[g]), axis=0, keepdims=True)
                    right_ref[pl.ds(rpos_ref[pairs[g]], 1), :] = top
                return carry

            lax.fori_loop(0, (high - low + GROUP - 1) // GROUP, block, 0)
            return carry

        lax.fori_loop(0, LEFTS, expert, 0)

    return pl.pallas_call(
        kernel,
        grid_spec=pltpu.PrefetchScalarGridSpec(
            num_scalar_prefetch=5,
            grid=(1,),
            in_specs=[ANY] * (1 + count),
            out_specs=[VMEM, VMEM],
            scratch_shapes=[
                pltpu.VMEM((LEFTS, ROWS, UNITS), jnp.bfloat16),
                pltpu.VMEM((NZ * NC * LEFTS, WIDTH, ROWS), jnp.bfloat16),
                pltpu.VMEM((LEFTS, UNITS), jnp.float32),
                pltpu.SemaphoreType.DMA((NX * NY + count,)),
            ],
        ),
        out_shape=[
            jax.ShapeDtypeStruct((NX * NY * SLOTS, QUARTER), jnp.float32),
            jax.ShapeDtypeStruct((NDEV * NX, WIDTH), jnp.float32),
        ],
        compiler_params=pltpu.CompilerParams(vmem_limit_bytes=48 << 20),
        name="correlate",
    )(start, order, jidx, lpos, rpos, gathered, *chunks)


def finish_right(rows, returned):
    def kernel(rows_ref, in_ref, out_ref):
        for s in range(SLOTS):
            for x in range(NX):
                out_ref[s : s + 1, x * WIDTH : (x + 1) * WIDTH] = in_ref[x, pl.ds(rows_ref[s], 1), :]

    return pl.pallas_call(
        kernel,
        grid_spec=pltpu.PrefetchScalarGridSpec(
            num_scalar_prefetch=1, grid=(1,), in_specs=[VMEM], out_specs=VMEM
        ),
        out_shape=jax.ShapeDtypeStruct((SLOTS, QUARTER), jnp.float32),
        name="finish_right",
    )(rows, returned)


def shift(value, axis, by, size):
    return lax.ppermute(value, axis, [(i, (i + by) % size) for i in range(size)])


def swap(value):
    return lax.ppermute(value, "core", [(0, 1), (1, 0)])


def body(unit_codes, block_scales, pair_list):
    x = lax.axis_index("x")
    z = lax.axis_index("z")
    c = lax.axis_index("core")
    me = (x * NZ + z) * NC + c

    table = pair_list.reshape(NX, NZ * NC, SLOTS, 2)
    mine = lax.dynamic_index_in_dim(table, z * NC + c, 1, keepdims=False).reshape(PAIRS, 2)
    pair = jnp.arange(PAIRS, dtype=jnp.int32)
    left_index = (pair // SLOTS) * PER + mine[:, 0] % PER
    right_dev = mine[:, 1] // PER
    right_x = right_dev // (NZ * NC)
    right_z = (right_dev // NC) % NZ
    right_c = right_dev % NC
    jidx = (((right_c != c) * NZ + (right_z - z) % NZ) * NX + right_x) * PER + mine[:, 1] % PER
    before = (left_index[None, :] < left_index[:, None]) | (
        (left_index[None, :] == left_index[:, None]) & (pair[None, :] < pair[:, None])
    )
    rank = jnp.sum(before, axis=1, dtype=jnp.int32)
    order = jnp.sum(jnp.where(rank[None, :] == pair[:, None], pair[None, :], 0), axis=1)
    start = jnp.sum(
        left_index[None, :] < jnp.arange(LEFTS + 1, dtype=jnp.int32)[:, None],
        axis=1,
        dtype=jnp.int32,
    )
    lpos = (pair // SLOTS) * (NY * SLOTS) + pair % SLOTS
    rpos = right_dev * NX + pair // SLOTS
    offsets = pair_list[:SLOTS, 1] // PER
    source = (me - offsets) % NDEV
    rows = (source % (NZ * NC)) * NX + source // (NZ * NC)

    acts, slices = prepare(unit_codes, block_scales)
    gathered = lax.all_gather(acts, ("x", "dp"), axis=0, tiled=False)
    pieces = lax.all_to_all(slices, ("dp", "x"), split_axis=0, concat_axis=0, tiled=True)
    own = normalise(pieces)

    half = LEFTS // 2
    chunks, places = [], []

    def keep(value, rel, first=0):
        for other, part in enumerate((value, swap(value))):
            chunks.append(part)
            places.append(((other * NZ + rel) * LEFTS + first, value.shape[0]))

    keep(own, 0)
    up = down = own
    for k in range(1, NZ // 2):
        up = shift(up, "z", 1, NZ)
        down = shift(down, "z", -1, NZ)
        keep(up, NZ - k)
        keep(down, k)
    keep(shift(up[:half], "z", 1, NZ), NZ // 2, 0)
    keep(shift(down[half:], "z", -1, NZ), NZ // 2, half)

    left, right = correlate(start, order, jidx, lpos, rpos, gathered, chunks, places)
    returned = lax.all_to_all(
        right.reshape(NDEV, NX, WIDTH), ("x", "z", "core"), split_axis=0, concat_axis=0, tiled=True
    )
    right_out = finish_right(rows, returned.reshape(NX, NZ * NC * NX, WIDTH))
    spread = lax.all_to_all(
        left.reshape(NX * NY, SLOTS, QUARTER), ("x", "dp"), split_axis=0, concat_axis=0, tiled=True
    )
    left_out = jnp.max(spread, axis=0)
    return (left_out[None], right_out[None])


def solution(mesh):
    fine = Mesh(np.asarray(mesh.devices).reshape(NY, NX, NZ, NC), ("dp", "x", "z", "core"))
    expert = ("x", "z", "core")
    in_specs = (P(expert, "dp", None), P(expert, None, "dp"), P())
    out_specs = (P(expert, None, "dp"), P(expert, None, "dp"))
    return jax.shard_map(body, mesh=fine, in_specs=in_specs, out_specs=out_specs, check_vma=False)
```

```python
import math

import jax
import jax.numpy as jnp
import numpy as np
from jax import lax
from jax.experimental import pallas as pl
from jax.experimental.pallas import tpu as pltpu
from jax.sharding import Mesh
from jax.sharding import PartitionSpec as P

EPSILON = 1e-06

NX, NZ, NC, NY = 4, 8, 2, 4
NDEV = NX * NZ * NC
PER = 2
ROWS = 256
RB = ROWS // NY
UNITS = 1536
SLICES = NX * NY
WIDTH = UNITS // SLICES
QUARTER = UNITS // NY
SLOTS = 32
PAIRS = NX * SLOTS
LEFTS = NX * PER
BLOCK = 128
GROUP = 8
TILE = 256

VMEM = pl.BlockSpec(memory_space=pltpu.VMEM)
HBM = pl.BlockSpec(memory_space=pltpu.HBM)


def prepare(codes, scales):
    def kernel(codes_ref, scales_ref, acts_ref, slices_ref):
        column = [jnp.transpose(scales_ref[h]) for h in range(PER)]
        for k in range(UNITS // BLOCK):
            lanes = slice(k * BLOCK, (k + 1) * BLOCK)
            both = []
            for h in range(PER):
                value = codes_ref[h, :, lanes].astype(jnp.float32) * column[h][:, k : k + 1]
                rounded = value.astype(jnp.bfloat16)
                acts_ref[h, :, lanes] = rounded
                both.append(rounded.astype(jnp.float32))
            turned = jnp.transpose(jnp.concatenate(both, axis=0)).astype(jnp.bfloat16)
            done = 0
            while done < BLOCK:
                unit = k * BLOCK + done
                take = min(BLOCK - done, WIDTH - unit % WIDTH)
                slices_ref[unit // WIDTH, unit % WIDTH : unit % WIDTH + take, :] = turned[
                    done : done + take
                ]
                done += take

    return pl.pallas_call(
        kernel,
        in_specs=[VMEM, VMEM],
        out_specs=[VMEM, VMEM],
        out_shape=[
            jax.ShapeDtypeStruct((PER, RB, UNITS), jnp.bfloat16),
            jax.ShapeDtypeStruct((SLICES, WIDTH, PER * RB), jnp.bfloat16),
        ],
        name="prepare",
    )(codes, scales)


def normalise(pieces):
    def kernel(in_ref, out_ref):
        for x in range(NX):
            part = [in_ref[y * NX + x].astype(jnp.float32) for y in range(NY)]
            for h in range(PER):
                lanes = slice(h * RB, (h + 1) * RB)
                full = jnp.concatenate([p[:, lanes] for p in part], axis=1)
                square = jnp.sum(full * full, axis=1, keepdims=True) / ROWS
                inverse = 1.0 / jnp.sqrt(square + EPSILON)
                out_ref[x * PER + h] = (full * (inverse * (1.0 / ROWS))).astype(jnp.bfloat16)

    return pl.pallas_call(
        kernel,
        in_specs=[VMEM],
        out_specs=VMEM,
        out_shape=jax.ShapeDtypeStruct((LEFTS, WIDTH, ROWS), jnp.bfloat16),
        name="normalise",
    )(pieces)


def correlate(start, order, jidx, lpos, rpos, gathered, chunks, places):
    count = len(chunks)

    def kernel(start_ref, order_ref, jidx_ref, lpos_ref, rpos_ref, *refs):
        gathered_ref = refs[0]
        chunk_refs = refs[1 : 1 + count]
        left_refs = refs[1 + count : 1 + count + NX * NY]
        right_ref, left, acts, others, inv, sem = refs[1 + count + NX * NY :]
        copies = []
        for x in range(NX):
            for y in range(NY):
                copies.append(
                    pltpu.make_async_copy(
                        gathered_ref.at[x * NY + y],
                        acts.at[pl.ds(x * PER, PER), pl.ds(y * RB, RB), :],
                        sem.at[len(copies)],
                    )
                )
        for ref, (at, size) in zip(chunk_refs, places):
            copies.append(
                pltpu.make_async_copy(ref, others.at[pl.ds(at, size)], sem.at[len(copies)])
            )
        for copy in copies:
            copy.start()
        right_ref[...] = jnp.zeros_like(right_ref)
        for copy in copies[: NX * NY]:
            copy.wait()

        def norm(i, carry):
            for n in range(UNITS // TILE):
                lanes = slice(n * TILE, (n + 1) * TILE)
                value = acts[i, :, lanes].astype(jnp.float32)
                square = jnp.sum(value * value, axis=0, keepdims=True) / ROWS
                inv[pl.ds(i, 1), lanes] = 1.0 / jnp.sqrt(square + EPSILON)
            return carry

        lax.fori_loop(0, LEFTS, norm, 0)
        for copy in copies[NX * NY :]:
            copy.wait()

        def expert(i, carry):
            low = start_ref[i]
            high = start_ref[i + 1]
            scales = inv[pl.ds(i, 1), :]

            def block(b, carry):
                pairs = [
                    order_ref[jnp.minimum(low + b * GROUP + g, high - 1)] for g in range(GROUP)
                ]
                lhs = jnp.concatenate([others[jidx_ref[p]] for p in pairs], axis=0)
                best = [None] * GROUP
                tops = [[] for _ in range(GROUP)]
                for n in range(UNITS // TILE):
                    out = jnp.dot(
                        lhs,
                        acts[i, :, n * TILE : (n + 1) * TILE],
                        preferred_element_type=jnp.float32,
                    )
                    for g in range(GROUP):
                        one = out[g * WIDTH : (g + 1) * WIDTH]
                        for m in range(TILE // 128):
                            unit = n * TILE + m * 128
                            scale = scales[:, unit : unit + 128]
                            part = one[:, m * 128 : (m + 1) * 128]
                            tops[g].append(jnp.max(part, axis=0, keepdims=True) * scale)
                            if (unit + 128) % QUARTER == 0:
                                row = lpos_ref[unit // QUARTER, pairs[g]]
                                left[pl.ds(row, 1), :] = jnp.concatenate(tops[g], axis=1)
                                tops[g] = []
                            scaled = part * scale
                            best[g] = scaled if best[g] is None else jnp.maximum(best[g], scaled)
                for g in range(GROUP):
                    top = jnp.max(jnp.transpose(best[g]), axis=0, keepdims=True)
                    right_ref[pl.ds(rpos_ref[pairs[g]], 1), :] = top
                return carry

            lax.fori_loop(0, (high - low + GROUP - 1) // GROUP, block, 0)
            return carry

        lax.fori_loop(0, LEFTS, expert, 0)
        for k in range(NX * NY):
            left_refs[k][...] = left[k * SLOTS : (k + 1) * SLOTS, :]

    return pl.pallas_call(
        kernel,
        grid_spec=pltpu.PrefetchScalarGridSpec(
            num_scalar_prefetch=5,
            grid=(1,),
            in_specs=[HBM] * (1 + count),
            out_specs=[VMEM] * (NX * NY + 1),
            scratch_shapes=[
                pltpu.VMEM((NX * NY * SLOTS, QUARTER), jnp.float32),
                pltpu.VMEM((LEFTS, ROWS, UNITS), jnp.bfloat16),
                pltpu.VMEM((NZ * NC * LEFTS, WIDTH, ROWS), jnp.bfloat16),
                pltpu.VMEM((LEFTS, UNITS), jnp.float32),
                pltpu.SemaphoreType.DMA((NX * NY + count,)),
            ],
        ),
        out_shape=[jax.ShapeDtypeStruct((SLOTS, QUARTER), jnp.float32)] * (NX * NY)
        + [jax.ShapeDtypeStruct((NDEV * NX, WIDTH), jnp.float32)],
        compiler_params=pltpu.CompilerParams(vmem_limit_bytes=48 << 20),
        name="correlate",
    )(start, order, jidx, lpos, rpos, gathered, *chunks)


def finish_right(rows, returned):
    def kernel(rows_ref, in_ref, out_ref):
        for s in range(SLOTS):
            for x in range(NX):
                out_ref[s : s + 1, x * WIDTH : (x + 1) * WIDTH] = in_ref[x, pl.ds(rows_ref[s], 1), :]

    return pl.pallas_call(
        kernel,
        grid_spec=pltpu.PrefetchScalarGridSpec(
            num_scalar_prefetch=1, grid=(1,), in_specs=[VMEM], out_specs=VMEM
        ),
        out_shape=jax.ShapeDtypeStruct((SLOTS, QUARTER), jnp.float32),
        name="finish_right",
    )(rows, returned)


def shift(value, axis, by, size):
    return lax.ppermute(value, axis, [(i, (i + by) % size) for i in range(size)])


def swap(value):
    return lax.ppermute(value, "core", [(0, 1), (1, 0)])


def body(unit_codes, block_scales, pair_list):
    y = lax.axis_index("dp")
    x = lax.axis_index("x")
    z = lax.axis_index("z")
    c = lax.axis_index("core")
    me = (x * NZ + z) * NC + c

    table = pair_list.reshape(NX, NZ * NC, SLOTS, 2)
    mine = lax.dynamic_index_in_dim(table, z * NC + c, 1, keepdims=False).reshape(PAIRS, 2)
    pair = jnp.arange(PAIRS, dtype=jnp.int32)
    left_index = (pair // SLOTS) * PER + mine[:, 0] % PER
    right_dev = mine[:, 1] // PER
    right_x = right_dev // (NZ * NC)
    right_z = (right_dev // NC) % NZ
    right_c = right_dev % NC
    jidx = (((right_c != c) * NZ + (right_z - z) % NZ) * NX + right_x) * PER + mine[:, 1] % PER
    before = (left_index[None, :] < left_index[:, None]) | (
        (left_index[None, :] == left_index[:, None]) & (pair[None, :] < pair[:, None])
    )
    rank = jnp.sum(before, axis=1, dtype=jnp.int32)
    order = jnp.sum(jnp.where(rank[None, :] == pair[:, None], pair[None, :], 0), axis=1)
    start = jnp.sum(
        left_index[None, :] < jnp.arange(LEFTS + 1, dtype=jnp.int32)[:, None],
        axis=1,
        dtype=jnp.int32,
    )
    quarter = jnp.arange(NY, dtype=jnp.int32)[:, None]
    away = ((pair // SLOTS - x) % NX)[None, :] * NY + (quarter - y) % NY
    lpos = away * SLOTS + (pair % SLOTS)[None, :]
    rpos = right_dev * NX + pair // SLOTS
    offsets = pair_list[:SLOTS, 1] // PER
    source = (me - offsets) % NDEV
    rows = (source % (NZ * NC)) * NX + source // (NZ * NC)

    acts, slices = prepare(unit_codes, block_scales)
    gathered = lax.all_gather(acts, ("x", "dp"), axis=0, tiled=False)
    pieces = lax.all_to_all(slices, ("dp", "x"), split_axis=0, concat_axis=0, tiled=True)
    own = normalise(pieces)

    half = LEFTS // 2
    chunks, places = [], []

    def keep(value, rel, first=0):
        for other, part in enumerate((value, swap(value))):
            chunks.append(part)
            places.append(((other * NZ + rel) * LEFTS + first, value.shape[0]))

    keep(own, 0)
    up = down = own
    for k in range(1, NZ // 2):
        up = shift(up, "z", 1, NZ)
        down = shift(down, "z", -1, NZ)
        keep(up, NZ - k)
        keep(down, k)
    keep(shift(up[:half], "z", 1, NZ), NZ // 2, 0)
    keep(shift(down[half:], "z", -1, NZ), NZ // 2, half)

    chunks = [pltpu.with_memory_space_constraint(v, pltpu.HBM) for v in chunks]
    *lefts, right = correlate(start, order, jidx, lpos, rpos, gathered, chunks, places)
    returned = lax.all_to_all(
        right.reshape(NDEV, NX, WIDTH), ("x", "z", "core"), split_axis=0, concat_axis=0, tiled=True
    )
    left_out = lefts[0]
    for k in range(1, NX * NY):
        dx, dy = divmod(k, NY)
        moves = [
            (j * NX + i, (j + dy) % NY * NX + (i + dx) % NX) for j in range(NY) for i in range(NX)
        ]
        left_out = jnp.maximum(left_out, lax.ppermute(lefts[k], ("dp", "x"), moves))
    right_out = finish_right(rows, returned.reshape(NX, NZ * NC * NX, WIDTH))
    return (left_out[None], right_out[None])


def solution(mesh):
    fine = Mesh(np.asarray(mesh.devices).reshape(NY, NX, NZ, NC), ("dp", "x", "z", "core"))
    expert = ("x", "z", "core")
    in_specs = (P(expert, "dp", None), P(expert, None, "dp"), P())
    out_specs = (P(expert, None, "dp"), P(expert, None, "dp"))
    return jax.shard_map(body, mesh=fine, in_specs=in_specs, out_specs=out_specs, check_vma=False)
```

```python
import jax
import jax.numpy as jnp
import numpy as np
from jax import lax
from jax.experimental import pallas as pl
from jax.experimental.pallas import tpu as pltpu
from jax.sharding import Mesh
from jax.sharding import PartitionSpec as P

EPSILON = 1e-06

NX, NZ, NC, NY = 4, 8, 2, 4
NDEV = NX * NZ * NC
PER = 2
ROWS = 256
RB = ROWS // NY
UNITS = 1536
SLICES = NX * NY
WIDTH = UNITS // SLICES
QUARTER = UNITS // NY
SLOTS = 32
QROWS = QUARTER // 128 * SLOTS
LROWS = NY * QROWS
PAIRS = NX * SLOTS
LEFTS = NX * PER
BLOCK = 128
HALF = LEFTS // 2
GROUP = 8
TILE = 256

VMEM = pl.BlockSpec(memory_space=pltpu.VMEM)
HBM = pl.BlockSpec(memory_space=pltpu.HBM)


def prepare(codes, scales):
    def kernel(codes_ref, scales_ref, acts_ref, slices_ref):
        column = [jnp.transpose(scales_ref[:, h, :]) for h in range(PER)]
        for k in range(UNITS // BLOCK):
            low = k * BLOCK
            both = []
            for h in range(PER):
                value = codes_ref[h, :, low : low + BLOCK].astype(jnp.float32)
                rounded = (value * column[h][:, k : k + 1]).astype(jnp.bfloat16)
                acts_ref[h, :, low : low + BLOCK] = rounded
                both.append(rounded.astype(jnp.float32))
            turned = jnp.transpose(jnp.concatenate(both, axis=0)).astype(jnp.bfloat16)
            done = 0
            while done < BLOCK:
                unit = low + done
                take = min(BLOCK - done, WIDTH - unit % WIDTH)
                slices_ref[unit // WIDTH, unit % WIDTH : unit % WIDTH + take, :] = turned[
                    done : done + take
                ]
                done += take

    return pl.pallas_call(
        kernel,
        in_specs=[VMEM, VMEM],
        out_specs=[VMEM] * 2,
        out_shape=[
            jax.ShapeDtypeStruct((PER, RB, UNITS), jnp.bfloat16),
            jax.ShapeDtypeStruct((SLICES, WIDTH, PER * RB), jnp.bfloat16),
        ],
        name="prepare",
    )(codes, scales)


def normalise(pieces):
    def kernel(in_ref, *out_refs):
        for x in range(NX):
            part = [in_ref[y * NX + x].astype(jnp.float32) for y in range(NY)]
            for h in range(PER):
                lanes = slice(h * RB, (h + 1) * RB)
                full = jnp.concatenate([p[:, lanes] for p in part], axis=1)
                square = jnp.sum(full * full, axis=1, keepdims=True) / ROWS
                inverse = 1.0 / jnp.sqrt(square + EPSILON)
                at = x * PER + h
                out_refs[at // HALF][at % HALF] = (full * (inverse * (1.0 / ROWS))).astype(jnp.bfloat16)

    return pl.pallas_call(
        kernel,
        in_specs=[VMEM],
        out_specs=[VMEM] * 2,
        out_shape=[jax.ShapeDtypeStruct((HALF, WIDTH, ROWS), jnp.bfloat16)] * 2,
        name="normalise",
    )(pieces)


def correlate(start, order, jidx, lpos, rpos, gathered, chunks, places):
    count = len(chunks)

    def kernel(start_ref, order_ref, jidx_ref, lpos_ref, rpos_ref, gathered_ref, *refs):
        chunk_refs = refs[:count]
        left_refs = refs[count : count + NX]
        right_ref, left, acts, others, norms, sem = refs[count + NX :]
        loads = [
            pltpu.make_async_copy(ref, others.at[pl.ds(at, size)], sem.at[n])
            for n, (ref, (at, size)) in enumerate(zip(chunk_refs, places))
        ]

        def rows_of(x, y):
            return pltpu.make_async_copy(
                gathered_ref.at[x * NY + y],
                acts.at[pl.ds(x * PER, PER), pl.ds(y * RB, RB), :],
                sem.at[count + x * NY + y],
            )

        for load in loads:
            load.start()
        for x in range(NX):
            for y in range(NY):
                rows_of(x, y).start()
        right_ref[...] = jnp.zeros_like(right_ref)
        for load in loads:
            load.wait()

        def expert(i, carry):
            @pl.when(i % PER == 0)
            def _():
                for y in range(NY):
                    rows_of(i // PER, y).wait()

            for n in range(UNITS // TILE):
                lanes = slice(n * TILE, (n + 1) * TILE)
                value = acts[i, :, lanes].astype(jnp.float32)
                square = jnp.sum(value * value, axis=0, keepdims=True) / ROWS
                norms[:, lanes] = 1.0 / jnp.sqrt(square + EPSILON)
            low = start_ref[i]
            high = start_ref[i + 1]
            scales = norms[...]

            def block(first, size):
                pairs = [order_ref[jnp.minimum(first + g, high - 1)] for g in range(size)]
                lhs = jnp.concatenate([others[jidx_ref[p]] for p in pairs], axis=0)
                best = [None] * size
                for n in range(UNITS // TILE):
                    out = jnp.dot(
                        lhs,
                        acts[i, :, n * TILE : (n + 1) * TILE],
                        preferred_element_type=jnp.float32,
                    )
                    for g in range(size):
                        one = out[g * WIDTH : (g + 1) * WIDTH]
                        for m in range(TILE // 128):
                            unit = n * TILE + m * 128
                            scale = scales[:, unit : unit + 128]
                            part = one[:, m * 128 : (m + 1) * 128]
                            top = jnp.max(part, axis=0, keepdims=True) * scale
                            row = lpos_ref[unit // QUARTER, pairs[g]] + unit % QUARTER // 128 * SLOTS
                            left[pl.ds(row, 1), :] = top
                            scaled = part * scale
                            best[g] = scaled if best[g] is None else jnp.maximum(best[g], scaled)
                for g in range(size):
                    top = jnp.max(jnp.transpose(best[g]), axis=0, keepdims=True)
                    right_ref[pl.ds(rpos_ref[pairs[g]], 1), :] = top

            rest = (high - low) % GROUP
            full = (high - low) // GROUP + (rest > GROUP // 2).astype(jnp.int32)

            def step(b, carry):
                block(low + b * GROUP, GROUP)
                return carry

            lax.fori_loop(0, full, step, 0)

            @pl.when((rest > 0) & (rest <= GROUP // 2))
            def _():
                block(low + full * GROUP, GROUP // 2)

            return carry

        lax.fori_loop(0, LEFTS, expert, 0)
        for k, ref in enumerate(left_refs):
            ref[...] = left[k * LROWS : (k + 1) * LROWS, :]

    return pl.pallas_call(
        kernel,
        grid_spec=pltpu.PrefetchScalarGridSpec(
            num_scalar_prefetch=5,
            grid=(1,),
            in_specs=[HBM] * (1 + count),
            out_specs=[VMEM] * (NX + 1),
            scratch_shapes=[
                pltpu.VMEM((NX * LROWS, 128), jnp.float32),
                pltpu.VMEM((LEFTS, ROWS, UNITS), jnp.bfloat16),
                pltpu.VMEM((NZ * NC * LEFTS, WIDTH, ROWS), jnp.bfloat16),
                pltpu.VMEM((1, UNITS), jnp.float32),
                pltpu.SemaphoreType.DMA((count + NX * NY,)),
            ],
        ),
        out_shape=[jax.ShapeDtypeStruct((LROWS, 128), jnp.float32)] * NX
        + [jax.ShapeDtypeStruct((NDEV * NX, WIDTH), jnp.float32)],
        compiler_params=pltpu.CompilerParams(vmem_limit_bytes=24 << 20),
        name="correlate",
    )(start, order, jidx, lpos, rpos, gathered, *chunks)


def finish_right(rows, returned):
    def kernel(rows_ref, in_ref, out_ref):
        for s in range(SLOTS):
            for x in range(NX):
                out_ref[s : s + 1, x * WIDTH : (x + 1) * WIDTH] = in_ref[x, pl.ds(rows_ref[s], 1), :]

    return pl.pallas_call(
        kernel,
        grid_spec=pltpu.PrefetchScalarGridSpec(
            num_scalar_prefetch=1, grid=(1,), in_specs=[VMEM], out_specs=VMEM
        ),
        out_shape=jax.ShapeDtypeStruct((SLOTS, QUARTER), jnp.float32),
        name="finish_right",
    )(rows, returned)


def meet(parts):
    def kernel(*refs):
        for k in range(NY):
            rows = slice(k * QROWS, (k + 1) * QROWS)
            best = refs[0][rows, :]
            for ref in refs[1:NX]:
                best = jnp.maximum(best, ref[rows, :])
            refs[NX + k][...] = best

    return pl.pallas_call(
        kernel,
        in_specs=[VMEM] * NX,
        out_specs=[VMEM] * NY,
        out_shape=[jax.ShapeDtypeStruct((QROWS, 128), jnp.float32)] * NY,
        name="meet",
    )(*parts)


def finish_left(parts):
    def kernel(*refs):
        for t in range(QUARTER // 128):
            rows = slice(t * SLOTS, (t + 1) * SLOTS)
            best = refs[0][rows, :]
            for ref in refs[1:NY]:
                best = jnp.maximum(best, ref[rows, :])
            refs[NY][:, t * 128 : (t + 1) * 128] = best

    return pl.pallas_call(
        kernel,
        in_specs=[VMEM] * NY,
        out_specs=VMEM,
        out_shape=jax.ShapeDtypeStruct((SLOTS, QUARTER), jnp.float32),
        name="finish_left",
    )(*parts)


def in_hbm(value):
    return pltpu.with_memory_space_constraint(value, pltpu.HBM)


def shift(value, axis, by, size):
    return lax.ppermute(value, axis, [(i, (i + by) % size) for i in range(size)])


def swap(value):
    return lax.ppermute(value, "core", [(0, 1), (1, 0)])


def body(unit_codes, block_scales, pair_list):
    y = lax.axis_index("dp")
    x = lax.axis_index("x")
    z = lax.axis_index("z")
    c = lax.axis_index("core")
    me = (x * NZ + z) * NC + c

    table = pair_list.reshape(NX, NZ * NC, SLOTS, 2)
    mine = lax.dynamic_index_in_dim(table, z * NC + c, 1, keepdims=False).reshape(PAIRS, 2)
    pair = jnp.arange(PAIRS, dtype=jnp.int32)
    right_dev = mine[:, 1] // PER
    right_x = right_dev // (NZ * NC)
    right_z = (right_dev // NC) % NZ
    right_c = right_dev % NC
    jidx = (((right_c != c) * NZ + (right_z - z) % NZ) * NX + right_x) * PER + mine[:, 1] % PER
    key = (pair // SLOTS) * PER + mine[:, 0] % PER
    before = (key[None, :] < key[:, None]) | (
        (key[None, :] == key[:, None]) & (pair[None, :] < pair[:, None])
    )
    rank = jnp.sum(before, axis=1, dtype=jnp.int32)
    order = jnp.sum(jnp.where(rank[None, :] == pair[:, None], pair[None, :], 0), axis=1)
    start = jnp.sum(
        key[None, :] < jnp.arange(LEFTS + 1, dtype=jnp.int32)[:, None], axis=1, dtype=jnp.int32
    )
    quarter = jnp.arange(NY, dtype=jnp.int32)[:, None]
    lpos = ((pair // SLOTS - x) % NX * LROWS + pair % SLOTS)[None, :] + (quarter - y) % NY * QROWS
    rpos = right_dev * NX + pair // SLOTS
    offsets = pair_list[:SLOTS, 1] // PER
    source = (me - offsets) % NDEV
    rows = (source % (NZ * NC)) * NX + source // (NZ * NC)

    acts, slices = prepare(unit_codes, jnp.transpose(block_scales, (1, 0, 2)))
    pieces = lax.all_to_all(slices, ("dp", "x"), split_axis=0, concat_axis=0, tiled=True)
    gathered = in_hbm(lax.all_gather(acts, ("x", "dp"), axis=0, tiled=False))
    own = normalise(pieces)

    chunks, places = [], []

    def keep(value, rel, chain):
        for other, part in enumerate((value, swap(value))):
            chunks.append(in_hbm(part))
            places.append(((other * NZ + rel) * LEFTS + chain * HALF, HALF))

    up, down = list(own), list(own)
    for chain in range(2):
        keep(own[chain], 0, chain)
    for k in range(1, NZ // 2):
        for chain in range(2):
            up[chain] = shift(up[chain], "z", 1, NZ)
            down[chain] = shift(down[chain], "z", -1, NZ)
        for chain in range(2):
            keep(up[chain], NZ - k, chain)
            keep(down[chain], k, chain)
    keep(shift(up[0], "z", 1, NZ), NZ // 2, 0)
    keep(shift(down[1], "z", -1, NZ), NZ // 2, 1)

    *left, right = correlate(start, order, jidx, lpos, rpos, gathered, chunks, places)
    returned = lax.all_to_all(
        right.reshape(NDEV, NX, WIDTH), ("x", "z", "core"), split_axis=0, concat_axis=0, tiled=True
    )
    right_out = finish_right(rows, returned.reshape(NX, NZ * NC * NX, WIDTH))
    parts = meet([left[0]] + [shift(left[k], "x", k, NX) for k in range(1, NX)])
    left_out = finish_left([parts[0]] + [shift(parts[k], "dp", k, NY) for k in range(1, NY)])
    return (left_out[None], right_out[None])


def solution(mesh):
    fine = Mesh(np.asarray(mesh.devices).reshape(NY, NX, NZ, NC), ("dp", "x", "z", "core"))
    expert = ("x", "z", "core")
    in_specs = (P(expert, "dp", None), P(expert, None, "dp"), P())
    out_specs = (P(expert, None, "dp"), P(expert, None, "dp"))
    return jax.shard_map(body, mesh=fine, in_specs=in_specs, out_specs=out_specs, check_vma=False)
```

```python
import jax
import jax.numpy as jnp
import numpy as np
from jax import lax
from jax.experimental import pallas as pl
from jax.experimental.pallas import tpu as pltpu
from jax.sharding import Mesh
from jax.sharding import PartitionSpec as P

EPSILON = 1e-06

NX, NZ, NC, NY = 4, 8, 2, 4
NDEV = NX * NZ * NC
PER = 2
ROWS = 256
RB = ROWS // NY
UNITS = 1536
SLICES = NX * NY
WIDTH = UNITS // SLICES
QUARTER = UNITS // NY
SLOTS = 32
QROWS = QUARTER // 128 * SLOTS
LROWS = NY * QROWS
PAIRS = NX * SLOTS
LEFTS = NX * PER
BLOCK = 128
HALF = LEFTS // 2
GROUP = 16
TILE = 256

VMEM = pl.BlockSpec(memory_space=pltpu.VMEM)
HBM = pl.BlockSpec(memory_space=pltpu.HBM)


def prepare(codes, scales):
    def kernel(codes_ref, scales_ref, acts_ref, slices_ref):
        column = [jnp.transpose(scales_ref[:, h, :]) for h in range(PER)]
        for k in range(UNITS // BLOCK):
            low = k * BLOCK
            both = []
            for h in range(PER):
                value = codes_ref[h, :, low : low + BLOCK].astype(jnp.float32)
                rounded = (value * column[h][:, k : k + 1]).astype(jnp.bfloat16)
                acts_ref[h, :, low : low + BLOCK] = rounded
                both.append(rounded.astype(jnp.float32))
            turned = jnp.transpose(jnp.concatenate(both, axis=0)).astype(jnp.bfloat16)
            done = 0
            while done < BLOCK:
                unit = low + done
                take = min(BLOCK - done, WIDTH - unit % WIDTH)
                slices_ref[unit // WIDTH, unit % WIDTH : unit % WIDTH + take, :] = turned[
                    done : done + take
                ]
                done += take

    return pl.pallas_call(
        kernel,
        in_specs=[VMEM, VMEM],
        out_specs=[VMEM] * 2,
        out_shape=[
            jax.ShapeDtypeStruct((PER, RB, UNITS), jnp.bfloat16),
            jax.ShapeDtypeStruct((SLICES, WIDTH, PER * RB), jnp.bfloat16),
        ],
        name="prepare",
    )(codes, scales)


def normalise(pieces):
    def kernel(in_ref, *out_refs):
        for x in range(NX):
            part = [in_ref[y * NX + x].astype(jnp.float32) for y in range(NY)]
            for h in range(PER):
                lanes = slice(h * RB, (h + 1) * RB)
                full = jnp.concatenate([p[:, lanes] for p in part], axis=1)
                square = jnp.sum(full * full, axis=1, keepdims=True) / ROWS
                inverse = 1.0 / jnp.sqrt(square + EPSILON)
                at = x * PER + h
                out_refs[at // HALF][at % HALF] = (full * (inverse * (1.0 / ROWS))).astype(jnp.bfloat16)

    return pl.pallas_call(
        kernel,
        in_specs=[VMEM],
        out_specs=[VMEM] * 2,
        out_shape=[jax.ShapeDtypeStruct((HALF, WIDTH, ROWS), jnp.bfloat16)] * 2,
        name="normalise",
    )(pieces)


def correlate(start, order, jidx, lpos, rpos, gathered, chunks, places):
    count = len(chunks)

    def kernel(start_ref, order_ref, jidx_ref, lpos_ref, rpos_ref, gathered_ref, *refs):
        chunk_refs = refs[:count]
        left_refs = refs[count : count + NX]
        right_ref, left, acts, others, norms, sem = refs[count + NX :]
        loads = [
            pltpu.make_async_copy(ref, others.at[pl.ds(at, size)], sem.at[n])
            for n, (ref, (at, size)) in enumerate(zip(chunk_refs, places))
        ]

        def rows_of(x, y):
            return pltpu.make_async_copy(
                gathered_ref.at[x * NY + y],
                acts.at[pl.ds(x * PER, PER), pl.ds(y * RB, RB), :],
                sem.at[count + x * NY + y],
            )

        for y in range(NY):
            rows_of(0, y).start()
        for load in loads:
            load.start()
        for x in range(1, NX):
            for y in range(NY):
                rows_of(x, y).start()
        right_ref[...] = jnp.zeros_like(right_ref)
        for load in loads:
            load.wait()

        def expert(i, carry):
            @pl.when(i % PER == 0)
            def _():
                for y in range(NY):
                    rows_of(i // PER, y).wait()

            for n in range(UNITS // TILE):
                lanes = slice(n * TILE, (n + 1) * TILE)
                value = acts[i, :, lanes].astype(jnp.float32)
                square = jnp.sum(value * value, axis=0, keepdims=True) / ROWS
                norms[:, lanes] = 1.0 / jnp.sqrt(square + EPSILON)
            low = start_ref[i]
            high = start_ref[i + 1]
            scales = norms[...]

            def block(first, size):
                pairs = [order_ref[jnp.minimum(first + g, high - 1)] for g in range(size)]
                lhs = jnp.concatenate([others[jidx_ref[p]] for p in pairs], axis=0)
                best = [None] * size
                for n in range(UNITS // TILE):
                    out = jnp.dot(
                        lhs,
                        acts[i, :, n * TILE : (n + 1) * TILE],
                        preferred_element_type=jnp.float32,
                    )
                    for g in range(size):
                        one = out[g * WIDTH : (g + 1) * WIDTH]
                        for m in range(TILE // 128):
                            unit = n * TILE + m * 128
                            scale = scales[:, unit : unit + 128]
                            part = one[:, m * 128 : (m + 1) * 128]
                            top = jnp.max(part, axis=0, keepdims=True) * scale
                            row = lpos_ref[unit // QUARTER, pairs[g]] + unit % QUARTER // 128 * SLOTS
                            left[pl.ds(row, 1), :] = top
                            scaled = part * scale
                            best[g] = scaled if best[g] is None else jnp.maximum(best[g], scaled)
                for g in range(size):
                    top = jnp.max(jnp.transpose(best[g]), axis=0, keepdims=True)
                    right_ref[pl.ds(rpos_ref[pairs[g]], 1), :] = top

            total = high - low
            rest = total % GROUP
            most = total // GROUP + (rest > 12).astype(jnp.int32)
            rest = jnp.where(rest > 12, 0, rest)
            eight = (rest > 4).astype(jnp.int32)

            def step(b, carry):
                block(low + b * GROUP, GROUP)
                return carry

            lax.fori_loop(0, most, step, 0)

            @pl.when(eight > 0)
            def _():
                block(low + most * GROUP, 8)

            @pl.when(rest - 8 * eight > 0)
            def _():
                block(low + most * GROUP + 8 * eight, 4)

            return carry

        lax.fori_loop(0, LEFTS, expert, 0)
        for k, ref in enumerate(left_refs):
            ref[...] = left[k * LROWS : (k + 1) * LROWS, :]

    return pl.pallas_call(
        kernel,
        grid_spec=pltpu.PrefetchScalarGridSpec(
            num_scalar_prefetch=5,
            grid=(1,),
            in_specs=[HBM] * (1 + count),
            out_specs=[VMEM] * (NX + 1),
            scratch_shapes=[
                pltpu.VMEM((NX * LROWS, 128), jnp.float32),
                pltpu.VMEM((LEFTS, ROWS, UNITS), jnp.bfloat16),
                pltpu.VMEM((NZ * NC * LEFTS, WIDTH, ROWS), jnp.bfloat16),
                pltpu.VMEM((1, UNITS), jnp.float32),
                pltpu.SemaphoreType.DMA((count + NX * NY,)),
            ],
        ),
        out_shape=[jax.ShapeDtypeStruct((LROWS, 128), jnp.float32)] * NX
        + [jax.ShapeDtypeStruct((NDEV * NX, WIDTH), jnp.float32)],
        compiler_params=pltpu.CompilerParams(vmem_limit_bytes=24 << 20),
        name="correlate",
    )(start, order, jidx, lpos, rpos, gathered, *chunks)


def finish(rows, returned, parts):
    def kernel(rows_ref, in_ref, *refs):
        part_refs, (left_ref, right_ref, picked) = refs[:NY], refs[NY:]
        for x in range(NX):
            for s in range(SLOTS):
                picked[x, s : s + 1, :] = in_ref[x, pl.ds(rows_ref[s], 1), :]
            right_ref[:, x * WIDTH : (x + 1) * WIDTH] = picked[x]
        for t in range(QUARTER // 128):
            some = slice(t * SLOTS, (t + 1) * SLOTS)
            best = part_refs[0][some, :]
            for ref in part_refs[1:]:
                best = jnp.maximum(best, ref[some, :])
            left_ref[:, t * 128 : (t + 1) * 128] = best

    return pl.pallas_call(
        kernel,
        grid_spec=pltpu.PrefetchScalarGridSpec(
            num_scalar_prefetch=1,
            grid=(1,),
            in_specs=[VMEM] * (1 + NY),
            out_specs=[VMEM] * 2,
            scratch_shapes=[pltpu.VMEM((NX, SLOTS, WIDTH), jnp.float32)],
        ),
        out_shape=[jax.ShapeDtypeStruct((SLOTS, QUARTER), jnp.float32)] * 2,
        name="finish",
    )(rows, returned, *parts)


def meet(parts):
    def kernel(*refs):
        for k in range(NY):
            rows = slice(k * QROWS, (k + 1) * QROWS)
            best = refs[0][rows, :]
            for ref in refs[1:NX]:
                best = jnp.maximum(best, ref[rows, :])
            refs[NX + k][...] = best

    return pl.pallas_call(
        kernel,
        in_specs=[VMEM] * NX,
        out_specs=[VMEM] * NY,
        out_shape=[jax.ShapeDtypeStruct((QROWS, 128), jnp.float32)] * NY,
        name="meet",
    )(*parts)


def in_hbm(value):
    return pltpu.with_memory_space_constraint(value, pltpu.HBM)


def in_vmem(value):
    return pltpu.with_memory_space_constraint(value, pltpu.VMEM)


def shift(value, axis, by, size):
    return lax.ppermute(value, axis, [(i, (i + by) % size) for i in range(size)])


def swap(value):
    return lax.ppermute(value, "core", [(0, 1), (1, 0)])


def body(unit_codes, block_scales, pair_list):
    y = lax.axis_index("dp")
    x = lax.axis_index("x")
    z = lax.axis_index("z")
    c = lax.axis_index("core")
    me = (x * NZ + z) * NC + c

    table = pair_list.reshape(NX, NZ * NC, SLOTS, 2)
    mine = lax.dynamic_index_in_dim(table, z * NC + c, 1, keepdims=False).reshape(PAIRS, 2)
    pair = jnp.arange(PAIRS, dtype=jnp.int32)
    right_dev = mine[:, 1] // PER
    right_x = right_dev // (NZ * NC)
    right_z = (right_dev // NC) % NZ
    right_c = right_dev % NC
    jidx = (((right_c != c) * NZ + (right_z - z) % NZ) * NX + right_x) * PER + mine[:, 1] % PER
    key = (pair // SLOTS) * PER + mine[:, 0] % PER
    before = (key[None, :] < key[:, None]) | (
        (key[None, :] == key[:, None]) & (pair[None, :] < pair[:, None])
    )
    rank = jnp.sum(before, axis=1, dtype=jnp.int32)
    order = jnp.sum(jnp.where(rank[None, :] == pair[:, None], pair[None, :], 0), axis=1)
    start = jnp.sum(
        key[None, :] < jnp.arange(LEFTS + 1, dtype=jnp.int32)[:, None], axis=1, dtype=jnp.int32
    )
    quarter = jnp.arange(NY, dtype=jnp.int32)[:, None]
    lpos = ((pair // SLOTS - x) % NX * LROWS + pair % SLOTS)[None, :] + (quarter - y) % NY * QROWS
    rpos = right_dev * NX + pair // SLOTS
    offsets = pair_list[:SLOTS, 1] // PER
    source = (me - offsets) % NDEV
    rows = (source % (NZ * NC)) * NX + source // (NZ * NC)

    acts, slices = prepare(unit_codes, jnp.transpose(block_scales, (1, 0, 2)))
    pieces = lax.all_to_all(slices, ("dp", "x"), split_axis=0, concat_axis=0, tiled=True)
    gathered = in_hbm(lax.all_gather(acts, ("x", "dp"), axis=0, tiled=False))
    own = normalise(pieces)

    chunks, places = [], []

    def keep(value, rel, chain):
        for other, part in enumerate((value, swap(value))):
            chunks.append(in_hbm(part))
            places.append(((other * NZ + rel) * LEFTS + chain * HALF, HALF))

    up, down = list(own), list(own)
    for chain in range(2):
        keep(own[chain], 0, chain)
    for k in range(1, NZ // 2):
        for chain in range(2):
            up[chain] = shift(up[chain], "z", 1, NZ)
            down[chain] = shift(down[chain], "z", -1, NZ)
        for chain in range(2):
            keep(up[chain], NZ - k, chain)
            keep(down[chain], k, chain)
    keep(shift(up[0], "z", 1, NZ), NZ // 2, 0)
    keep(shift(down[1], "z", -1, NZ), NZ // 2, 1)

    order, rows = lax.optimization_barrier((order, rows))
    *left, right = correlate(start, order, jidx, lpos, rpos, gathered, chunks, places)
    returned = lax.all_to_all(
        right.reshape(NDEV, NX, WIDTH), ("x", "z", "core"), split_axis=0, concat_axis=0, tiled=True
    )
    parts = meet([left[0]] + [in_vmem(shift(left[k], "x", k, NX)) for k in range(1, NX)])
    parts = [parts[0]] + [in_vmem(shift(parts[k], "dp", k, NY)) for k in range(1, NY)]
    returned = in_vmem(returned.reshape(NX, NZ * NC * NX, WIDTH))
    left_out, right_out = finish(rows, returned, parts)
    return (left_out[None], right_out[None])


def solution(mesh):
    fine = Mesh(np.asarray(mesh.devices).reshape(NY, NX, NZ, NC), ("dp", "x", "z", "core"))
    expert = ("x", "z", "core")
    in_specs = (P(expert, "dp", None), P(expert, None, "dp"), P())
    out_specs = (P(expert, None, "dp"), P(expert, None, "dp"))
    return jax.shard_map(body, mesh=fine, in_specs=in_specs, out_specs=out_specs, check_vma=False)
```

```python
import jax
import jax.numpy as jnp
import numpy as np
from jax import lax
from jax.experimental import pallas as pl
from jax.experimental.pallas import tpu as pltpu
from jax.sharding import Mesh
from jax.sharding import PartitionSpec as P

EPSILON = 1e-06

NX, NZ, NC, NY = 4, 8, 2, 4
NDEV = NX * NZ * NC
PER = 2
ROWS = 256
RB = ROWS // NY
UNITS = 1536
QUARTER = UNITS // NY
SLOTS = 32
QROWS = QUARTER // 128 * SLOTS
LEFTS = NX * PER
BLOCK = 128
GROUP = 4
TILE = 256

VMEM = pl.BlockSpec(memory_space=pltpu.VMEM)
HBM = pl.BlockSpec(memory_space=pltpu.HBM)


def prepare(codes, scales):
    def kernel(codes_ref, scales_ref, acts_ref, slices_ref):
        column = [jnp.transpose(scales_ref[:, h, :]) for h in range(PER)]
        for k in range(UNITS // BLOCK):
            low = k * BLOCK
            both = []
            for h in range(PER):
                value = codes_ref[h, :, low : low + BLOCK].astype(jnp.float32)
                rounded = (value * column[h][:, k : k + 1]).astype(jnp.bfloat16)
                acts_ref[h, :, low : low + BLOCK] = rounded
                both.append(rounded.astype(jnp.float32))
            turned = jnp.transpose(jnp.concatenate(both, axis=0)).astype(jnp.bfloat16)
            first = low % QUARTER
            slices_ref[low // QUARTER, first : first + BLOCK, :] = turned

    return pl.pallas_call(
        kernel,
        in_specs=[VMEM, VMEM],
        out_specs=[VMEM] * 2,
        out_shape=[
            jax.ShapeDtypeStruct((PER, RB, UNITS), jnp.bfloat16),
            jax.ShapeDtypeStruct((NY, QUARTER, PER * RB), jnp.bfloat16),
        ],
        name="prepare",
    )(codes, scales)


def normalise(pieces):
    def kernel(in_ref, *out_refs):
        for k in range(QUARTER // 128):
            units = slice(k * 128, (k + 1) * 128)
            part = [in_ref[y, units, :].astype(jnp.float32) for y in range(NY)]
            for h in range(PER):
                lanes = slice(h * RB, (h + 1) * RB)
                full = jnp.concatenate([p[:, lanes] for p in part], axis=1)
                square = jnp.sum(full * full, axis=1, keepdims=True) / ROWS
                inverse = 1.0 / jnp.sqrt(square + EPSILON)
                out_refs[h][units, :] = (full * (inverse * (1.0 / ROWS))).astype(jnp.bfloat16)

    return pl.pallas_call(
        kernel,
        in_specs=[VMEM],
        out_specs=[VMEM] * PER,
        out_shape=[jax.ShapeDtypeStruct((QUARTER, ROWS), jnp.bfloat16)] * PER,
        name="normalise",
    )(pieces)


def correlate(start, order, jidx, lpos, rpos, gathered, chunks, places):
    count = len(chunks)

    def kernel(start_ref, order_ref, jidx_ref, lpos_ref, rpos_ref, gathered_ref, *refs):
        chunk_refs = refs[:count]
        left_refs = refs[count : count + NY]
        right_ref, left, acts, others, norms, sem = refs[count + NY :]
        loads = [
            pltpu.make_async_copy(ref, others.at[at], sem.at[n])
            for n, (ref, at) in enumerate(zip(chunk_refs, places))
        ]

        def rows_of(x, y):
            return pltpu.make_async_copy(
                gathered_ref.at[x * NY + y],
                acts.at[pl.ds(x * PER, PER), pl.ds(y * RB, RB), :],
                sem.at[count + x * NY + y],
            )

        for y in range(NY):
            rows_of(0, y).start()
        for load in loads:
            load.start()
        for x in range(1, NX):
            for y in range(NY):
                rows_of(x, y).start()
        right_ref[...] = jnp.zeros_like(right_ref)
        for load in loads:
            load.wait()

        def expert(i, carry):
            @pl.when(i % PER == 0)
            def _():
                for y in range(NY):
                    rows_of(i // PER, y).wait()

            for n in range(UNITS // TILE):
                lanes = slice(n * TILE, (n + 1) * TILE)
                value = acts[i, :, lanes].astype(jnp.float32)
                square = jnp.sum(value * value, axis=0, keepdims=True) / ROWS
                norms[:, lanes] = 1.0 / jnp.sqrt(square + EPSILON)
            low = start_ref[i]
            high = start_ref[i + 1]
            scales = norms[...]

            def block(first, size):
                pairs = [order_ref[first + g] for g in range(size)]
                lhs = jnp.concatenate([others[jidx_ref[p]] for p in pairs], axis=0)
                best = [None] * size
                for n in range(UNITS // TILE):
                    out = jnp.dot(
                        lhs,
                        acts[i, :, n * TILE : (n + 1) * TILE],
                        preferred_element_type=jnp.float32,
                    )
                    for g in range(size):
                        one = out[g * QUARTER : (g + 1) * QUARTER]
                        for m in range(TILE // 128):
                            unit = n * TILE + m * 128
                            scale = scales[:, unit : unit + 128]
                            part = one[:, m * 128 : (m + 1) * 128]
                            top = jnp.max(part, axis=0, keepdims=True) * scale
                            row = lpos_ref[unit // QUARTER, pairs[g]] + unit % QUARTER // 128 * SLOTS
                            left[pl.ds(row, 1), :] = top
                            scaled = part * scale
                            best[g] = scaled if best[g] is None else jnp.maximum(best[g], scaled)
                for g in range(size):
                    top = jnp.max(jnp.transpose(best[g]), axis=0, keepdims=True)
                    right_ref[pl.ds(rpos_ref[pairs[g]], 1), :] = top

            most = (high - low) // GROUP
            rest = (high - low) % GROUP
            two = rest // 2

            def step(b, carry):
                block(low + b * GROUP, GROUP)
                return carry

            lax.fori_loop(0, most, step, 0)

            @pl.when(two > 0)
            def _():
                block(low + most * GROUP, 2)

            @pl.when(rest % 2 > 0)
            def _():
                block(low + most * GROUP + 2 * two, 1)

            return carry

        lax.fori_loop(0, LEFTS, expert, 0)
        for k, ref in enumerate(left_refs):
            ref[...] = left[k * QROWS : (k + 1) * QROWS, :]

    return pl.pallas_call(
        kernel,
        grid_spec=pltpu.PrefetchScalarGridSpec(
            num_scalar_prefetch=5,
            grid=(1,),
            in_specs=[HBM] * (1 + count),
            out_specs=[VMEM] * (NY + 1),
            scratch_shapes=[
                pltpu.VMEM((NY * QROWS, 128), jnp.float32),
                pltpu.VMEM((LEFTS, ROWS, UNITS), jnp.bfloat16),
                pltpu.VMEM((NZ * NC * PER, QUARTER, ROWS), jnp.bfloat16),
                pltpu.VMEM((1, UNITS), jnp.float32),
                pltpu.SemaphoreType.DMA((count + NX * NY,)),
            ],
        ),
        out_shape=[jax.ShapeDtypeStruct((QROWS, 128), jnp.float32)] * NY
        + [jax.ShapeDtypeStruct((NZ * NC * NX, QUARTER), jnp.float32)],
        compiler_params=pltpu.CompilerParams(vmem_limit_bytes=24 << 20),
        name="correlate",
    )(start, order, jidx, lpos, rpos, gathered, *chunks)


def finish(rows, returned, choice, parts):
    def kernel(rows_ref, in_ref, choice_ref, *refs):
        part_refs, (left_ref, right_ref) = refs[:NX], refs[NX:]
        for s in range(SLOTS):
            right_ref[s : s + 1, :] = in_ref[pl.ds(rows_ref[s], 1), :]
        chosen = choice_ref[...]
        for t in range(QUARTER // 128):
            some = slice(t * SLOTS, (t + 1) * SLOTS)
            value = part_refs[0][some, :]
            for k in range(1, NX):
                value = jnp.where(chosen == k, part_refs[k][some, :], value)
            left_ref[:, t * 128 : (t + 1) * 128] = value

    return pl.pallas_call(
        kernel,
        grid_spec=pltpu.PrefetchScalarGridSpec(
            num_scalar_prefetch=1,
            grid=(1,),
            in_specs=[VMEM] * (2 + NX),
            out_specs=[VMEM] * 2,
        ),
        out_shape=[jax.ShapeDtypeStruct((SLOTS, QUARTER), jnp.float32)] * 2,
        name="finish",
    )(rows, returned, choice, *parts)


def meet(parts):
    def kernel(*refs):
        best = refs[0][...]
        for ref in refs[1:NY]:
            best = jnp.maximum(best, ref[...])
        refs[NY][...] = best

    return pl.pallas_call(
        kernel,
        in_specs=[VMEM] * NY,
        out_specs=VMEM,
        out_shape=jax.ShapeDtypeStruct((QROWS, 128), jnp.float32),
        name="meet",
    )(*parts)


def in_hbm(value):
    return pltpu.with_memory_space_constraint(value, pltpu.HBM)


def in_vmem(value):
    return pltpu.with_memory_space_constraint(value, pltpu.VMEM)


def shift(value, axis, by, size):
    return lax.ppermute(value, axis, [(i, (i + by) % size) for i in range(size)])


def swap(value):
    return lax.ppermute(value, "core", [(0, 1), (1, 0)])


def body(unit_codes, block_scales, pair_list):
    y = lax.axis_index("dp")
    x = lax.axis_index("x")
    z = lax.axis_index("z")
    c = lax.axis_index("core")
    me = (x * NZ + z) * NC + c

    table = pair_list.reshape(NX, NZ * NC, SLOTS, 2)
    group = lax.dynamic_index_in_dim(table, z * NC + c, 1, keepdims=False)
    group_x = group[:, :, 1] // (PER * NZ * NC)
    here = group_x == x
    mine = jnp.sum(jnp.where(here[:, :, None], group, 0), axis=0)
    pair = jnp.arange(SLOTS, dtype=jnp.int32)
    left_x = mine[:, 0] // (PER * NZ * NC)
    right_dev = mine[:, 1] // PER
    right_z = (right_dev // NC) % NZ
    right_c = right_dev % NC
    jidx = ((right_c != c) * NZ + (right_z - z) % NZ) * PER + mine[:, 1] % PER
    key = left_x * PER + mine[:, 0] % PER
    before = (key[None, :] < key[:, None]) | (
        (key[None, :] == key[:, None]) & (pair[None, :] < pair[:, None])
    )
    rank = jnp.sum(before, axis=1, dtype=jnp.int32)
    order = jnp.sum(jnp.where(rank[None, :] == pair[:, None], pair[None, :], 0), axis=1)
    start = jnp.sum(
        key[None, :] < jnp.arange(LEFTS + 1, dtype=jnp.int32)[:, None], axis=1, dtype=jnp.int32
    )
    quarter = jnp.arange(NY, dtype=jnp.int32)[:, None]
    lpos = pair[None, :] + (quarter - y) % NY * QROWS
    rpos = (right_z * NC + right_c) * NX + left_x
    own_x = lax.dynamic_index_in_dim(group_x, x, 0, keepdims=False)
    choice = jnp.broadcast_to(((x - own_x) % NX)[:, None], (SLOTS, 128))
    offsets = pair_list[:SLOTS, 1] // PER
    source = (me - offsets) % NDEV
    rows = (source % (NZ * NC)) * NX + source // (NZ * NC)

    acts, slices = prepare(unit_codes, jnp.transpose(block_scales, (1, 0, 2)))
    pieces = lax.all_to_all(slices, "dp", split_axis=0, concat_axis=0, tiled=True)
    gathered = in_hbm(lax.all_gather(acts, ("x", "dp"), axis=0, tiled=False))
    own = normalise(pieces)

    chunks, places = [], []

    def keep(value, rel, h):
        for other, part in enumerate((value, swap(value))):
            chunks.append(in_hbm(part))
            places.append((other * NZ + rel) * PER + h)

    up, down = list(own), list(own)
    for h in range(PER):
        keep(own[h], 0, h)
    for k in range(1, NZ // 2):
        for h in range(PER):
            up[h] = shift(up[h], "z", 1, NZ)
            down[h] = shift(down[h], "z", -1, NZ)
        for h in range(PER):
            keep(up[h], NZ - k, h)
            keep(down[h], k, h)
    keep(shift(up[0], "z", 1, NZ), NZ // 2, 0)
    keep(shift(down[1], "z", -1, NZ), NZ // 2, 1)

    order, rows, choice = lax.optimization_barrier((order, rows, choice))
    *left, right = correlate(start, order, jidx, lpos, rpos, gathered, chunks, places)
    returned = lax.all_to_all(
        right.reshape(NZ * NC, NX, QUARTER), ("z", "core"), split_axis=0, concat_axis=0, tiled=True
    )
    best = meet([left[0]] + [in_vmem(shift(left[k], "dp", k, NY)) for k in range(1, NY)])
    parts = [best] + [in_vmem(shift(best, "x", k, NX)) for k in range(1, NX)]
    returned = in_vmem(returned.reshape(NZ * NC * NX, QUARTER))
    left_out, right_out = finish(rows, returned, choice, parts)
    return (left_out[None], right_out[None])


def solution(mesh):
    fine = Mesh(np.asarray(mesh.devices).reshape(NY, NX, NZ, NC), ("dp", "x", "z", "core"))
    expert = ("x", "z", "core")
    in_specs = (P(expert, "dp", None), P(expert, None, "dp"), P())
    out_specs = (P(expert, None, "dp"), P(expert, None, "dp"))
    return jax.shard_map(body, mesh=fine, in_specs=in_specs, out_specs=out_specs, check_vma=False)
```

```python
import jax
import jax.numpy as jnp
import numpy as np
from jax import lax
from jax.experimental import pallas as pl
from jax.experimental.pallas import tpu as pltpu
from jax.sharding import Mesh
from jax.sharding import PartitionSpec as P

EPSILON = 1e-06

NX, NZ, NC, NY = 4, 8, 2, 4
NDEV = NX * NZ * NC
PER = 2
ROWS = 256
RB = ROWS // NY
UNITS = 1536
QUARTER = UNITS // NY
SLOTS = 32
RSTEP = 8
QROWS = QUARTER // 128 * SLOTS
LEFTS = NX * PER
BLOCK = 128
GROUP = 4
TILE = 256

VMEM = pl.BlockSpec(memory_space=pltpu.VMEM)
HBM = pl.BlockSpec(memory_space=pltpu.HBM)


def prepare(codes, scales):
    def kernel(codes_ref, scales_ref, acts_ref):
        first = pl.program_id(0) == 0
        column = jnp.transpose(jnp.where(first, scales_ref[:, 0, :], scales_ref[:, 1, :]))
        for k in range(UNITS // BLOCK):
            lanes = slice(k * BLOCK, (k + 1) * BLOCK)
            value = codes_ref[0, :, lanes].astype(jnp.float32) * column[:, k : k + 1]
            acts_ref[0, :, lanes] = value.astype(jnp.bfloat16)

    one = pl.BlockSpec((1, RB, UNITS), lambda h: (h, 0, 0))
    return pl.pallas_call(
        kernel,
        grid=(PER,),
        in_specs=[one, pl.BlockSpec((UNITS // BLOCK, PER, RB), lambda h: (0, 0, 0))],
        out_specs=one,
        out_shape=jax.ShapeDtypeStruct((PER, RB, UNITS), jnp.bfloat16),
        name="prepare",
    )(codes, scales)


def turn(acts):
    def kernel(acts_ref, slices_ref):
        for k in range(UNITS // BLOCK):
            low = k * BLOCK
            both = [acts_ref[h, :, low : low + BLOCK].astype(jnp.float32) for h in range(PER)]
            turned = jnp.transpose(jnp.concatenate(both, axis=0)).astype(jnp.bfloat16)
            first = low % QUARTER
            slices_ref[low // QUARTER, first : first + BLOCK, :] = turned

    return pl.pallas_call(
        kernel,
        in_specs=[VMEM],
        out_specs=VMEM,
        out_shape=jax.ShapeDtypeStruct((NY, QUARTER, PER * RB), jnp.bfloat16),
        name="turn",
    )(acts)


def normalise(pieces):
    def kernel(in_ref, *out_refs):
        for k in range(QUARTER // 128):
            units = slice(k * 128, (k + 1) * 128)
            part = [in_ref[y, units, :].astype(jnp.float32) for y in range(NY)]
            for h in range(PER):
                lanes = slice(h * RB, (h + 1) * RB)
                full = jnp.concatenate([p[:, lanes] for p in part], axis=1)
                square = jnp.sum(full * full, axis=1, keepdims=True) / ROWS
                inverse = 1.0 / jnp.sqrt(square + EPSILON)
                out_refs[h][units, :] = (full * (inverse * (1.0 / ROWS))).astype(jnp.bfloat16)

    return pl.pallas_call(
        kernel,
        in_specs=[VMEM],
        out_specs=[VMEM] * PER,
        out_shape=[jax.ShapeDtypeStruct((QUARTER, ROWS), jnp.bfloat16)] * PER,
        name="normalise",
    )(pieces)


def correlate(start, order, jidx, lpos, rpos, gathered, chunks, places):
    count = len(chunks)

    def kernel(start_ref, order_ref, jidx_ref, lpos_ref, rpos_ref, gathered_ref, *refs):
        chunk_refs = refs[:count]
        left_refs = refs[count : count + NY]
        right_out, right_ref, left, acts, others, norms, sem, out_sem = refs[count + NY :]
        loads = [
            pltpu.make_async_copy(ref, others.at[at], sem.at[n])
            for n, (ref, at) in enumerate(zip(chunk_refs, places))
        ]

        def rows_of(x, y):
            return pltpu.make_async_copy(
                gathered_ref.at[x * NY + y],
                acts.at[pl.ds(x * PER, PER), pl.ds(y * RB, RB), :],
                sem.at[count + x * NY + y],
            )

        for y in range(NY):
            rows_of(0, y).start()
        for load in loads:
            load.start()
        for x in range(1, NX):
            for y in range(NY):
                rows_of(x, y).start()
        right_ref[...] = jnp.zeros_like(right_ref)

        def norm(x):
            for y in range(NY):
                rows_of(x, y).wait()
            for i in range(PER):
                for n in range(UNITS // TILE):
                    lanes = slice(n * TILE, (n + 1) * TILE)
                    value = acts[x * PER + i, :, lanes].astype(jnp.float32)
                    square = jnp.sum(value * value, axis=0, keepdims=True) / ROWS
                    norms[pl.ds(x * PER + i, 1), lanes] = 1.0 / jnp.sqrt(square + EPSILON)

        norm(0)
        for load in loads:
            load.wait()

        def expert(i, carry):
            @pl.when((i % PER == 0) & (i > 0))
            def _():
                norm(i // PER)

            low = start_ref[i]
            high = start_ref[i + 1]
            scales = norms[pl.ds(i, 1), :]

            def block(first, size):
                pairs = [order_ref[first + g] for g in range(size)]
                lhs = jnp.concatenate([others[jidx_ref[p]] for p in pairs], axis=0)
                best = [None] * size
                for n in range(UNITS // TILE):
                    out = jnp.dot(
                        lhs,
                        acts[i, :, n * TILE : (n + 1) * TILE],
                        preferred_element_type=jnp.float32,
                    )
                    for g in range(size):
                        one = out[g * QUARTER : (g + 1) * QUARTER]
                        for m in range(TILE // 128):
                            unit = n * TILE + m * 128
                            scale = scales[:, unit : unit + 128]
                            part = one[:, m * 128 : (m + 1) * 128]
                            top = jnp.max(part, axis=0, keepdims=True) * scale
                            row = lpos_ref[unit // QUARTER, pairs[g]] + unit % QUARTER // 128 * SLOTS
                            left[pl.ds(row, 1), :] = top
                            scaled = part * scale
                            best[g] = scaled if best[g] is None else jnp.maximum(best[g], scaled)
                for g in range(size):
                    top = jnp.max(jnp.transpose(best[g]), axis=0, keepdims=True)
                    right_ref[pl.ds(rpos_ref[pairs[g]], 1), :] = top

            most = (high - low) // GROUP
            rest = (high - low) % GROUP
            two = rest // 2

            def step(b, carry):
                block(low + b * GROUP, GROUP)
                return carry

            lax.fori_loop(0, most, step, 0)

            @pl.when(two > 0)
            def _():
                block(low + most * GROUP, 2)

            @pl.when(rest % 2 > 0)
            def _():
                block(low + most * GROUP + 2 * two, 1)

            return carry

        lax.fori_loop(0, LEFTS, expert, 0)
        stores = [pltpu.make_async_copy(right_ref, right_out, out_sem.at[0])]
        for k in range(1, NY):
            some = left.at[pl.ds(k * QROWS, QROWS), :]
            stores.append(pltpu.make_async_copy(some, left_refs[k], out_sem.at[k]))
        for store in stores:
            store.start()
        left_refs[0][...] = left[:QROWS, :]
        for store in stores:
            store.wait()

    return pl.pallas_call(
        kernel,
        grid_spec=pltpu.PrefetchScalarGridSpec(
            num_scalar_prefetch=5,
            grid=(1,),
            in_specs=[HBM] * (1 + count),
            out_specs=[VMEM] + [HBM] * NY,
            scratch_shapes=[
                pltpu.VMEM((NZ * NC * RSTEP, QUARTER), jnp.float32),
                pltpu.VMEM((NY * QROWS, 128), jnp.float32),
                pltpu.VMEM((LEFTS, ROWS, UNITS), jnp.bfloat16),
                pltpu.VMEM((NZ * NC * PER, QUARTER, ROWS), jnp.bfloat16),
                pltpu.VMEM((LEFTS, UNITS), jnp.float32),
                pltpu.SemaphoreType.DMA((count + NX * NY,)),
                pltpu.SemaphoreType.DMA((NY,)),
            ],
        ),
        out_shape=[jax.ShapeDtypeStruct((QROWS, 128), jnp.float32)] * NY
        + [jax.ShapeDtypeStruct((NZ * NC * RSTEP, QUARTER), jnp.float32)],
        compiler_params=pltpu.CompilerParams(vmem_limit_bytes=24 << 20),
        name="correlate",
    )(start, order, jidx, lpos, rpos, gathered, *chunks)


def finish(rows, returned, choice, parts):
    def kernel(rows_ref, in_ref, choice_ref, *refs):
        part_refs, (left_ref, right_ref) = refs[:NX], refs[NX:]
        for s in range(SLOTS):
            right_ref[s : s + 1, :] = in_ref[pl.ds(rows_ref[s], 1), :]
        chosen = choice_ref[...]
        for t in range(QUARTER // 128):
            some = slice(t * SLOTS, (t + 1) * SLOTS)
            value = part_refs[0][some, :]
            for k in range(1, NX):
                value = jnp.where(chosen == k, part_refs[k][some, :], value)
            left_ref[:, t * 128 : (t + 1) * 128] = value

    return pl.pallas_call(
        kernel,
        grid_spec=pltpu.PrefetchScalarGridSpec(
            num_scalar_prefetch=1,
            grid=(1,),
            in_specs=[VMEM] * (2 + NX),
            out_specs=[VMEM] * 2,
        ),
        out_shape=[jax.ShapeDtypeStruct((SLOTS, QUARTER), jnp.float32)] * 2,
        name="finish",
    )(rows, returned, choice, *parts)


def meet(parts):
    def kernel(*refs):
        best = refs[0][...]
        for ref in refs[1:NY]:
            best = jnp.maximum(best, ref[...])
        refs[NY][...] = best

    return pl.pallas_call(
        kernel,
        in_specs=[VMEM] * NY,
        out_specs=VMEM,
        out_shape=jax.ShapeDtypeStruct((QROWS, 128), jnp.float32),
        name="meet",
    )(*parts)


def in_hbm(value):
    return pltpu.with_memory_space_constraint(value, pltpu.HBM)


def in_vmem(value):
    return pltpu.with_memory_space_constraint(value, pltpu.VMEM)


def shift(value, axis, by, size):
    return lax.ppermute(value, axis, [(i, (i + by) % size) for i in range(size)])


def swap(value):
    return lax.ppermute(value, "core", [(0, 1), (1, 0)])


def body(unit_codes, block_scales, pair_list):
    y = lax.axis_index("dp")
    x = lax.axis_index("x")
    z = lax.axis_index("z")
    c = lax.axis_index("core")
    me = (x * NZ + z) * NC + c

    table = pair_list.reshape(NX, NZ * NC, SLOTS, 2)
    group = lax.dynamic_index_in_dim(table, z * NC + c, 1, keepdims=False)
    group_x = group[:, :, 1] // (PER * NZ * NC)
    here = group_x == x
    mine = jnp.sum(jnp.where(here[:, :, None], group, 0), axis=0)
    pair = jnp.arange(SLOTS, dtype=jnp.int32)
    left_x = mine[:, 0] // (PER * NZ * NC)
    right_dev = mine[:, 1] // PER
    right_z = (right_dev // NC) % NZ
    right_c = right_dev % NC
    jidx = ((right_c != c) * NZ + (right_z - z) % NZ) * PER + mine[:, 1] % PER
    key = left_x * PER + mine[:, 0] % PER
    before = (key[None, :] < key[:, None]) | (
        (key[None, :] == key[:, None]) & (pair[None, :] < pair[:, None])
    )
    rank = jnp.sum(before, axis=1, dtype=jnp.int32)
    order = jnp.sum(jnp.where(rank[None, :] == pair[:, None], pair[None, :], 0), axis=1)
    start = jnp.sum(
        key[None, :] < jnp.arange(LEFTS + 1, dtype=jnp.int32)[:, None], axis=1, dtype=jnp.int32
    )
    quarter = jnp.arange(NY, dtype=jnp.int32)[:, None]
    lpos = pair[None, :] + (quarter - y) % NY * QROWS
    rpos = (right_z * NC + right_c) * RSTEP + left_x
    own_x = lax.dynamic_index_in_dim(group_x, x, 0, keepdims=False)
    choice = jnp.broadcast_to(((x - own_x) % NX)[:, None], (SLOTS, 128))
    offsets = pair_list[:SLOTS, 1] // PER
    source = (me - offsets) % NDEV
    rows = (source % (NZ * NC)) * RSTEP + source // (NZ * NC)

    acts = prepare(unit_codes, jnp.transpose(block_scales, (1, 0, 2)))
    slices = turn(acts)
    pieces = lax.all_to_all(slices, "dp", split_axis=0, concat_axis=0, tiled=True)
    gathered = in_hbm(lax.all_gather(acts, ("x", "dp"), axis=0, tiled=False))
    own = normalise(pieces)

    chunks, places = [], []

    def keep(value, rel, h):
        for other, part in enumerate((value, swap(value))):
            chunks.append(in_hbm(part))
            places.append((other * NZ + rel) * PER + h)

    up, down = list(own), list(own)
    for h in range(PER):
        keep(own[h], 0, h)
    for k in range(1, NZ // 2):
        for h in range(PER):
            up[h] = shift(up[h], "z", 1, NZ)
            down[h] = shift(down[h], "z", -1, NZ)
        for h in range(PER):
            keep(up[h], NZ - k, h)
            keep(down[h], k, h)
    keep(shift(up[0], "z", 1, NZ), NZ // 2, 0)
    keep(shift(down[1], "z", -1, NZ), NZ // 2, 1)

    order, rows, choice = lax.optimization_barrier((order, rows, choice))
    *left, right = correlate(start, order, jidx, lpos, rpos, gathered, chunks, places)
    returned = lax.all_to_all(
        right.reshape(NZ * NC, RSTEP, QUARTER), ("z", "core"), split_axis=0, concat_axis=0, tiled=True
    )
    best = meet([left[0]] + [in_vmem(shift(left[k], "dp", k, NY)) for k in range(1, NY)])
    parts = [best] + [in_vmem(shift(best, "x", k, NX)) for k in range(1, NX)]
    returned = in_vmem(returned.reshape(NZ * NC * RSTEP, QUARTER))
    left_out, right_out = finish(rows, returned, choice, parts)
    return (left_out[None], right_out[None])


def solution(mesh):
    fine = Mesh(np.asarray(mesh.devices).reshape(NY, NX, NZ, NC), ("dp", "x", "z", "core"))
    expert = ("x", "z", "core")
    in_specs = (P(expert, "dp", None), P(expert, None, "dp"), P())
    out_specs = (P(expert, None, "dp"), P(expert, None, "dp"))
    return jax.shard_map(body, mesh=fine, in_specs=in_specs, out_specs=out_specs, check_vma=False)
```

```python
import jax
import jax.numpy as jnp
import numpy as np
from jax import lax
from jax.experimental import pallas as pl
from jax.experimental.pallas import tpu as pltpu
from jax.sharding import Mesh
from jax.sharding import PartitionSpec as P

EPSILON = 1e-06

NX, NZ, NC, NY = 4, 8, 2, 4
NDEV = NX * NZ * NC
PER = 2
ROWS = 256
RB = ROWS // NY
UNITS = 1536
QUARTER = UNITS // NY
SLOTS = 32
RSTEP = 8
QROWS = QUARTER // 128 * SLOTS
LEFTS = NX * PER
BLOCK = 128
GROUP = 4
TILE = 512

VMEM = pl.BlockSpec(memory_space=pltpu.VMEM)
HBM = pl.BlockSpec(memory_space=pltpu.HBM)


def prepare(codes, scales):
    def kernel(codes_ref, scales_ref, acts_ref):
        first = pl.program_id(0) == 0
        column = jnp.transpose(jnp.where(first, scales_ref[:, 0, :], scales_ref[:, 1, :]))
        for k in range(UNITS // BLOCK):
            lanes = slice(k * BLOCK, (k + 1) * BLOCK)
            value = codes_ref[0, :, lanes].astype(jnp.float32) * column[:, k : k + 1]
            acts_ref[0, :, lanes] = value.astype(jnp.bfloat16)

    one = pl.BlockSpec((1, RB, UNITS), lambda h: (h, 0, 0))
    return pl.pallas_call(
        kernel,
        grid=(PER,),
        in_specs=[one, pl.BlockSpec((UNITS // BLOCK, PER, RB), lambda h: (0, 0, 0))],
        out_specs=one,
        out_shape=jax.ShapeDtypeStruct((PER, RB, UNITS), jnp.bfloat16),
        name="prepare",
    )(codes, scales)


def turn(acts):
    def kernel(acts_ref, slices_ref):
        for k in range(UNITS // BLOCK):
            low = k * BLOCK
            both = [acts_ref[h, :, low : low + BLOCK].astype(jnp.float32) for h in range(PER)]
            turned = jnp.transpose(jnp.concatenate(both, axis=0)).astype(jnp.bfloat16)
            first = low % QUARTER
            slices_ref[low // QUARTER, first : first + BLOCK, :] = turned

    return pl.pallas_call(
        kernel,
        in_specs=[VMEM],
        out_specs=VMEM,
        out_shape=jax.ShapeDtypeStruct((NY, QUARTER, PER * RB), jnp.bfloat16),
        name="turn",
    )(acts)


def normalise(pieces):
    def kernel(in_ref, *out_refs):
        for k in range(QUARTER // 128):
            units = slice(k * 128, (k + 1) * 128)
            part = [in_ref[y, units, :].astype(jnp.float32) for y in range(NY)]
            for h in range(PER):
                lanes = slice(h * RB, (h + 1) * RB)
                full = jnp.concatenate([p[:, lanes] for p in part], axis=1)
                square = jnp.sum(full * full, axis=1, keepdims=True) / ROWS
                inverse = 1.0 / jnp.sqrt(square + EPSILON)
                out_refs[h][units, :] = (full * (inverse * (1.0 / ROWS))).astype(jnp.bfloat16)

    return pl.pallas_call(
        kernel,
        in_specs=[VMEM],
        out_specs=[VMEM] * PER,
        out_shape=[jax.ShapeDtypeStruct((QUARTER, ROWS), jnp.bfloat16)] * PER,
        name="normalise",
    )(pieces)


def correlate(start, order, jidx, lpos, rpos, gathered, chunks, places):
    count = len(chunks)

    def kernel(start_ref, order_ref, jidx_ref, lpos_ref, rpos_ref, gathered_ref, *refs):
        chunk_refs = refs[:count]
        left_refs = refs[count : count + NY]
        right_out, right_ref, left, acts, others, norms, sem, out_sem = refs[count + NY :]
        loads = [
            pltpu.make_async_copy(ref, others.at[at], sem.at[n])
            for n, (ref, at) in enumerate(zip(chunk_refs, places))
        ]

        def rows_of(x, y):
            return pltpu.make_async_copy(
                gathered_ref.at[x * NY + y],
                acts.at[pl.ds(x * PER, PER), pl.ds(y * RB, RB), :],
                sem.at[count + x * NY + y],
            )

        for y in range(NY):
            rows_of(0, y).start()
        for load in loads:
            load.start()
        for x in range(1, NX):
            for y in range(NY):
                rows_of(x, y).start()
        right_ref[...] = jnp.zeros_like(right_ref)

        def norm(x):
            for y in range(NY):
                rows_of(x, y).wait()
            for i in range(PER):
                for n in range(UNITS // TILE):
                    lanes = slice(n * TILE, (n + 1) * TILE)
                    value = acts[x * PER + i, :, lanes].astype(jnp.float32)
                    square = jnp.sum(value * value, axis=0, keepdims=True) / ROWS
                    norms[pl.ds(x * PER + i, 1), lanes] = 1.0 / jnp.sqrt(square + EPSILON)

        norm(0)
        for load in loads:
            load.wait()

        def expert(i, carry):
            @pl.when((i % PER == 0) & (i > 0))
            def _():
                norm(i // PER)

            low = start_ref[i]
            high = start_ref[i + 1]
            scales = norms[pl.ds(i, 1), :]

            def block(first, size):
                pairs = [order_ref[first + g] for g in range(size)]
                lhs = jnp.concatenate([others[jidx_ref[p]] for p in pairs], axis=0)
                best = [None] * size
                for n in range(UNITS // TILE):
                    out = jnp.dot(
                        lhs,
                        acts[i, :, n * TILE : (n + 1) * TILE],
                        preferred_element_type=jnp.float32,
                    )
                    for g in range(size):
                        one = out[g * QUARTER : (g + 1) * QUARTER]
                        for m in range(TILE // 128):
                            unit = n * TILE + m * 128
                            scale = scales[:, unit : unit + 128]
                            part = one[:, m * 128 : (m + 1) * 128]
                            top = jnp.max(part, axis=0, keepdims=True) * scale
                            row = lpos_ref[unit // QUARTER, pairs[g]] + unit % QUARTER // 128 * SLOTS
                            left[pl.ds(row, 1), :] = top
                            scaled = part * scale
                            best[g] = scaled if best[g] is None else jnp.maximum(best[g], scaled)
                for g in range(size):
                    top = jnp.max(jnp.transpose(best[g]), axis=0, keepdims=True)
                    right_ref[pl.ds(rpos_ref[pairs[g]], 1), :] = top

            most = (high - low) // GROUP
            rest = (high - low) % GROUP
            two = rest // 2

            def step(b, carry):
                block(low + b * GROUP, GROUP)
                return carry

            lax.fori_loop(0, most, step, 0)

            @pl.when(two > 0)
            def _():
                block(low + most * GROUP, 2)

            @pl.when(rest % 2 > 0)
            def _():
                block(low + most * GROUP + 2 * two, 1)

            return carry

        lax.fori_loop(0, LEFTS, expert, 0)
        stores = [pltpu.make_async_copy(right_ref, right_out, out_sem.at[0])]
        for k in range(1, NY):
            some = left.at[pl.ds(k * QROWS, QROWS), :]
            stores.append(pltpu.make_async_copy(some, left_refs[k], out_sem.at[k]))
        for store in stores:
            store.start()
        left_refs[0][...] = left[:QROWS, :]
        for store in stores:
            store.wait()

    return pl.pallas_call(
        kernel,
        grid_spec=pltpu.PrefetchScalarGridSpec(
            num_scalar_prefetch=5,
            grid=(1,),
            in_specs=[HBM] * (1 + count),
            out_specs=[VMEM] + [HBM] * NY,
            scratch_shapes=[
                pltpu.VMEM((NZ * NC * RSTEP, QUARTER), jnp.float32),
                pltpu.VMEM((NY * QROWS, 128), jnp.float32),
                pltpu.VMEM((LEFTS, ROWS, UNITS), jnp.bfloat16),
                pltpu.VMEM((NZ * NC * PER, QUARTER, ROWS), jnp.bfloat16),
                pltpu.VMEM((LEFTS, UNITS), jnp.float32),
                pltpu.SemaphoreType.DMA((count + NX * NY,)),
                pltpu.SemaphoreType.DMA((NY,)),
            ],
        ),
        out_shape=[jax.ShapeDtypeStruct((QROWS, 128), jnp.float32)] * NY
        + [jax.ShapeDtypeStruct((NZ * NC * RSTEP, QUARTER), jnp.float32)],
        compiler_params=pltpu.CompilerParams(vmem_limit_bytes=24 << 20),
        name="correlate",
    )(start, order, jidx, lpos, rpos, gathered, *chunks)


def finish(rows, returned, choice, parts):
    def kernel(rows_ref, in_ref, choice_ref, *refs):
        part_refs, (left_ref, right_ref) = refs[:NX], refs[NX:]
        for s in range(SLOTS):
            right_ref[s : s + 1, :] = in_ref[pl.ds(rows_ref[s], 1), :]
        chosen = choice_ref[...]
        for t in range(QUARTER // 128):
            some = slice(t * SLOTS, (t + 1) * SLOTS)
            value = part_refs[0][some, :]
            for k in range(1, NX):
                value = jnp.where(chosen == k, part_refs[k][some, :], value)
            left_ref[:, t * 128 : (t + 1) * 128] = value

    return pl.pallas_call(
        kernel,
        grid_spec=pltpu.PrefetchScalarGridSpec(
            num_scalar_prefetch=1,
            grid=(1,),
            in_specs=[VMEM] * (2 + NX),
            out_specs=[VMEM] * 2,
        ),
        out_shape=[jax.ShapeDtypeStruct((SLOTS, QUARTER), jnp.float32)] * 2,
        name="finish",
    )(rows, returned, choice, *parts)


def meet(parts):
    def kernel(*refs):
        best = refs[0][...]
        for ref in refs[1:NY]:
            best = jnp.maximum(best, ref[...])
        refs[NY][...] = best

    return pl.pallas_call(
        kernel,
        in_specs=[VMEM] * NY,
        out_specs=VMEM,
        out_shape=jax.ShapeDtypeStruct((QROWS, 128), jnp.float32),
        name="meet",
    )(*parts)


def in_hbm(value):
    return pltpu.with_memory_space_constraint(value, pltpu.HBM)


def in_vmem(value):
    return pltpu.with_memory_space_constraint(value, pltpu.VMEM)


def shift(value, axis, by, size):
    return lax.ppermute(value, axis, [(i, (i + by) % size) for i in range(size)])


def swap(value):
    return lax.ppermute(value, "core", [(0, 1), (1, 0)])


def body(unit_codes, block_scales, pair_list):
    y = lax.axis_index("dp")
    x = lax.axis_index("x")
    z = lax.axis_index("z")
    c = lax.axis_index("core")
    me = (x * NZ + z) * NC + c

    table = pair_list.reshape(NX, NZ * NC, SLOTS, 2)
    group = lax.dynamic_index_in_dim(table, z * NC + c, 1, keepdims=False)
    group_x = group[:, :, 1] // (PER * NZ * NC)
    here = group_x == x
    mine = jnp.sum(jnp.where(here[:, :, None], group, 0), axis=0)
    pair = jnp.arange(SLOTS, dtype=jnp.int32)
    left_x = mine[:, 0] // (PER * NZ * NC)
    right_dev = mine[:, 1] // PER
    right_z = (right_dev // NC) % NZ
    right_c = right_dev % NC
    jidx = ((right_c != c) * NZ + (right_z - z) % NZ) * PER + mine[:, 1] % PER
    key = left_x * PER + mine[:, 0] % PER
    before = (key[None, :] < key[:, None]) | (
        (key[None, :] == key[:, None]) & (pair[None, :] < pair[:, None])
    )
    rank = jnp.sum(before, axis=1, dtype=jnp.int32)
    order = jnp.sum(jnp.where(rank[None, :] == pair[:, None], pair[None, :], 0), axis=1)
    start = jnp.sum(
        key[None, :] < jnp.arange(LEFTS + 1, dtype=jnp.int32)[:, None], axis=1, dtype=jnp.int32
    )
    quarter = jnp.arange(NY, dtype=jnp.int32)[:, None]
    lpos = pair[None, :] + (quarter - y) % NY * QROWS
    rpos = (right_z * NC + right_c) * RSTEP + left_x
    own_x = lax.dynamic_index_in_dim(group_x, x, 0, keepdims=False)
    choice = jnp.broadcast_to(((x - own_x) % NX)[:, None], (SLOTS, 128))
    offsets = pair_list[:SLOTS, 1] // PER
    source = (me - offsets) % NDEV
    rows = (source % (NZ * NC)) * RSTEP + source // (NZ * NC)

    acts = prepare(unit_codes, jnp.transpose(block_scales, (1, 0, 2)))
    slices = turn(acts)
    pieces = lax.all_to_all(slices, "dp", split_axis=0, concat_axis=0, tiled=True)
    gathered = in_hbm(lax.all_gather(acts, ("x", "dp"), axis=0, tiled=False))
    own = normalise(pieces)

    chunks, places = [], []

    def keep(value, rel, h):
        for other, part in enumerate((value, swap(value))):
            chunks.append(in_hbm(part))
            places.append((other * NZ + rel) * PER + h)

    up, down = list(own), list(own)
    for h in range(PER):
        keep(own[h], 0, h)
    for k in range(1, NZ // 2):
        for h in range(PER):
            up[h] = shift(up[h], "z", 1, NZ)
            down[h] = shift(down[h], "z", -1, NZ)
        for h in range(PER):
            keep(up[h], NZ - k, h)
            keep(down[h], k, h)
    keep(shift(up[0], "z", 1, NZ), NZ // 2, 0)
    keep(shift(down[1], "z", -1, NZ), NZ // 2, 1)

    order, rows, choice = lax.optimization_barrier((order, rows, choice))
    *left, right = correlate(start, order, jidx, lpos, rpos, gathered, chunks, places)
    returned = lax.all_to_all(
        right.reshape(NZ * NC, RSTEP, QUARTER), ("z", "core"), split_axis=0, concat_axis=0, tiled=True
    )
    best = meet([left[0]] + [in_vmem(shift(left[k], "dp", k, NY)) for k in range(1, NY)])
    parts = [best] + [in_vmem(shift(best, "x", k, NX)) for k in range(1, NX)]
    returned = in_vmem(returned.reshape(NZ * NC * RSTEP, QUARTER))
    left_out, right_out = finish(rows, returned, choice, parts)
    return (left_out[None], right_out[None])


def solution(mesh):
    fine = Mesh(np.asarray(mesh.devices).reshape(NY, NX, NZ, NC), ("dp", "x", "z", "core"))
    expert = ("x", "z", "core")
    in_specs = (P(expert, "dp", None), P(expert, None, "dp"), P())
    out_specs = (P(expert, None, "dp"), P(expert, None, "dp"))
    return jax.shard_map(body, mesh=fine, in_specs=in_specs, out_specs=out_specs, check_vma=False)
```
